32 devices in a mesh: member: 4 (over x, core), gx: 2 (over y), gy: 4 (over z).
Axes of the slice: x: 2, y: 2, z: 4, core: 2. Of those that a mesh axis runs over, the one named last changes fastest.
Arguments:
- tracers: float32 [8, 16, 128, 512], P('member', None, 'gx', 'gy'), may hold values from -6 to 6
- flux_x: float32 [16, 128, 512], P('member', 'gx', 'gy'), may hold values from -0.4 to 0.4
- flux_y: float32 [16, 128, 512], P('member', 'gx', 'gy'), may hold values from -0.4 to 0.4
- flux_z: float32 [16, 128, 512], P('member', 'gx', 'gy'), may hold values from -0.4 to 0.4
Outputs:
- transported: float32 [8, 16, 128, 512], P('member', None, 'gx', 'gy')
The draws below stay inside these ranges and needn't reach their ends.
All inputs are finite; a program needn't handle non-finite values.
Results may differ from the reference program's by a relative error of at most 0.0003.
Values sent between devices are 32-bit elements; how exact they have to be, the bound alone decides.
A program may use at most 128 MiB of HBM per device.

```python
import jax
import jax.numpy as jnp
from jax import lax

LEV = 16
TRACERS = 8
NX = 128
NY = 512


def block_scale(rng, extent, pieces, low, largest):
    factor_of = 1.0
    for position, blocks in pieces:
        draws = jax.random.uniform(jax.random.fold_in(jax.random.fold_in(rng, 6), position), (blocks,), jnp.float32, low / len(pieces), largest / len(pieces))
        factor_of = factor_of * jnp.repeat(jnp.exp(draws), extent[position] // blocks).reshape((-1,) + (1,) * (len(extent) - 1 - position))
    return factor_of


def noise(own_key, shape, scale, reach, shards=(), held_as=jnp.bfloat16):
    factor_of = block_scale(own_key, shape, shards, -0.22, 0.18) if shards else 1.0
    array = jax.random.normal(own_key, shape, jnp.float32) * scale * factor_of
    return jnp.minimum(jnp.maximum(array, -reach), reach).astype(held_as)


def setup_inputs(seed: int = 0) -> dict:
    splits = jax.random.split(jax.random.key(seed), 5)
    return {
        "tracers": noise(splits[0], (TRACERS, LEV, NX, NY), 1.0, 6.0, ((0, 4), (2, 2), (3, 4)), jnp.float32),
        "flux_x": jnp.clip(jax.random.uniform(splits[1], (LEV, NX, NY), jnp.float32, -0.4, 0.4) * block_scale(splits[1], (LEV, NX, NY), ((0, 4), (1, 2), (2, 4)), -0.4, 0.0), -0.4, 0.4),
        "flux_y": jnp.clip(jax.random.uniform(splits[2], (LEV, NX, NY), jnp.float32, -0.4, 0.4) * block_scale(splits[2], (LEV, NX, NY), ((0, 4), (1, 2), (2, 4)), -0.4, 0.0), -0.4, 0.4),
        "flux_z": jnp.clip(jax.random.uniform(splits[3], (LEV, NX, NY), jnp.float32, -0.4, 0.4) * block_scale(splits[3], (LEV, NX, NY), ((0, 4), (1, 2), (2, 4)), -0.4, 0.0), -0.4, 0.4),
    }


def advect(field, faces, axis):
    cells = faces.shape[axis] - 1

    def along(source, start, stop):
        return lax.slice_in_dim(source, start, stop, axis=axis)

    face_values = (7.0 * (along(field, 1, cells + 4) + along(field, 2, cells + 5)) - (along(field, 0, cells + 3) + along(field, 3, cells + 6))) / 12.0
    lower_a = along(face_values, 0, cells + 1)
    lower_b = along(face_values, 1, cells + 2)
    lower_mid = along(field, 2, cells + 3)
    upper_a = along(face_values, 1, cells + 2)
    upper_b = along(face_values, 2, cells + 3)
    upper_mid = along(field, 3, cells + 4)
    lower_d = lower_b - lower_a
    lower_h = 6.0 * lower_mid - 3.0 * (lower_a + lower_b)
    upper_d = upper_b - upper_a
    upper_h = 6.0 * upper_mid - 3.0 * (upper_a + upper_b)
    gauge = -faces
    from_lower = faces * (lower_b - 0.5 * faces * (lower_d - (1.0 - 2.0 * faces / 3.0) * lower_h))
    from_upper = faces * (upper_a + 0.5 * gauge * (upper_d + (1.0 - 2.0 * gauge / 3.0) * upper_h))
    face_flux = jnp.where(faces > 0, from_lower, from_upper)
    return along(field, 3, cells + 3) - (along(face_flux, 1, cells + 1) - along(face_flux, 0, cells))


def reference(tracers, flux_x, flux_y, flux_z):
    face_x = jnp.concatenate([flux_x[:, -1:, :], flux_x], axis=1)
    face_y = jnp.concatenate([flux_y[:, :, -1:], flux_y], axis=2)
    closed = jnp.zeros_like(flux_z[:1])
    face_z = jnp.concatenate([closed, flux_z[:-1], closed], axis=0)

    def advance(field):
        for step_index in range(2):
            field = advect(jnp.pad(field, ((0, 0), (3, 3), (0, 0)), mode="wrap"), face_x, 1)
            field = advect(jnp.pad(field, ((0, 0), (0, 0), (3, 3)), mode="wrap"), face_y, 2)
            field = advect(jnp.pad(field, ((3, 3), (0, 0), (0, 0)), mode="edge"), face_z, 0)
        return field

    return lax.map(advance, tracers)
```

```python
import functools

import jax
import jax.numpy as jnp
from jax import lax
from jax.experimental import pallas as pl
from jax.experimental.pallas import tpu as pltpu
from jax.sharding import PartitionSpec as P

MESH = pl.DeviceIdType.MESH
LANES = 128
GROUP = 8
RIM = 3
TAPS = 2 * RIM + 1
FACE = 2 * RIM


def coefficients(c):
    s = jnp.abs(c)
    t = 1.0 - s
    ct = c * t * (1.0 / 12.0)
    return c > 0, ct * t, ct * s, c * s * (3.0 - 2.0 * s)


def flux(coefs, e, o, upwind):
    _, near, far, mean = coefs
    return near * e - far * o + mean * upwind


def face_weights(c):
    positive, near, far, mean = coefficients(c)
    near7 = 7.0 * near
    far7 = 7.0 * far
    second = -(near + far7)
    upwind = near7 - far7 + mean
    downwind = near7 + far
    last = -near
    zero = jnp.zeros_like(c)
    return (
        jnp.where(positive, far, zero),
        jnp.where(positive, second, last),
        jnp.where(positive, upwind, downwind),
        jnp.where(positive, downwind, upwind),
        jnp.where(positive, last, second),
        jnp.where(positive, zero, far),
    )


def cell_taps(low, high):
    taps = [low[0]]
    for k in range(1, FACE):
        taps.append(low[k] - high[k - 1])
    taps.append(-high[FACE - 1])
    taps[RIM] = taps[RIM] + 1.0
    return taps


def weighted(taps, cells):
    terms = [a * b for a, b in zip(taps, cells)]
    while len(terms) > 1:
        terms = [sum(terms[i : i + 2]) if i + 1 < len(terms) else terms[i] for i in range(0, len(terms), 2)]
    return terms[0]


def kernel(
    sizes,
    tracers,
    flux_x,
    flux_y,
    flux_z,
    out,
    field0,
    field1,
    turned0,
    turned1,
    mid,
    fx,
    fy,
    fz,
    fyt,
    vx,
    vy,
    face,
    swept,
    local_sem,
    wind_send,
    wind_recv,
    edge_send,
    edge_recv,
    halo_send,
    halo_recv,
    pack_send,
    pack_recv,
):
    members, n_x, n_y = sizes
    trac, levels, width_x, width_y = tracers.shape
    slab = levels // members
    pairs = slab // 2
    m = lax.axis_index("member")
    ix = lax.axis_index("gx")
    iy = lax.axis_index("gy")

    def member_of(j):
        if j == 0:
            return m
        if j == 1:
            return m + 1 - 2 * lax.rem(m, 2)
        if j == 2:
            return lax.rem(m + 2, 4)
        return 3 - m

    def device(j, dx, dy):
        return (member_of(j), lax.rem(ix + dx + n_x, n_x), lax.rem(iy + dy + n_y, n_y))

    x_steps = (1,) if n_x == 2 else (1, -1)
    y_steps = (1,) if n_y == 2 else (1, -1)
    partners = [(1, 0, 0), (2, 0, 0)]
    partners += [(j, d, 0) for j in range(4) for d in x_steps]
    partners += [(j, 0, d) for j in range(4) for d in y_steps]
    barrier = pltpu.get_barrier_semaphore()
    for partner in partners:
        pl.semaphore_signal(barrier, inc=1, device_id=device(*partner), device_id_type=MESH)

    def levels_of(j):
        return pl.ds(member_of(j) * slab, slab)

    def pairs_of(j):
        return pl.ds(member_of(j) * pairs, pairs)

    inner = pl.ds(GROUP, width_x)
    winds = ((flux_x, fx), (flux_y, fy), (flux_z, fz))

    def wind_dst(k, j):
        if k == 0:
            return fx.at[levels_of(j), inner, :]
        return winds[k][1].at[levels_of(j), :, :]

    locals_ = [
        pltpu.make_async_copy(winds[k][0], wind_dst(k, 0), local_sem.at[k]) for k in range(3)
    ]
    load = pltpu.make_async_copy(tracers, field0.at[:, :, inner, :], local_sem.at[3])
    locals_[1].start()
    locals_[0].start()
    load.start()
    locals_[2].start()

    def remote(src, dst, send, recv, dev):
        return pltpu.make_async_remote_copy(
            src_ref=src, dst_ref=dst, send_sem=send, recv_sem=recv, device_id=dev, device_id_type=MESH
        )

    def halo_copies(step, j):
        target = (field0, field1)[step]
        ls = levels_of(j)
        if step == 0:
            low_src = tracers.at[:, ls, pl.ds(0, RIM), :]
            high_src = tracers.at[:, ls, pl.ds(width_x - RIM, RIM), :]
        else:
            low_src = field1.at[:, ls, pl.ds(GROUP, RIM), :]
            high_src = field1.at[:, ls, pl.ds(GROUP + width_x - RIM, RIM), :]
        return (
            remote(
                high_src,
                target.at[:, ls, pl.ds(GROUP - RIM, RIM), :],
                halo_send.at[step, j, 0],
                halo_recv.at[step, j, 0],
                device(0, 1, 0),
            ),
            remote(
                low_src,
                target.at[:, ls, pl.ds(width_x + GROUP, RIM), :],
                halo_send.at[step, j, 1],
                halo_recv.at[step, j, 1],
                device(0, -1, 0),
            ),
        )

    def pack_copies(step, j):
        turned = (turned0, turned1)[step]
        ps = pairs_of(j)
        return (
            remote(
                turned.at[:, ps, pl.ds(GROUP + width_y - RIM, RIM), :],
                turned.at[:, ps, pl.ds(GROUP - RIM, RIM), :],
                pack_send.at[step, j, 0],
                pack_recv.at[step, j, 0],
                device(0, 0, 1),
            ),
            remote(
                turned.at[:, ps, pl.ds(GROUP, RIM), :],
                turned.at[:, ps, pl.ds(GROUP + width_y, RIM), :],
                pack_send.at[step, j, 1],
                pack_recv.at[step, j, 1],
                device(0, 0, -1),
            ),
        )

    halos = [[halo_copies(step, j) for j in range(4)] for step in range(2)]
    packs = [[pack_copies(step, j) for j in range(4)] for step in range(2)]
    direct = [[remote(winds[k][0], wind_dst(k, 0), wind_send.at[j - 1, k], wind_recv.at[j - 1, k], device(j, 0, 0))
               for k in range(3)] for j in (1, 2)]
    relay = [
        remote(wind_dst(k, 2), wind_dst(k, 2), wind_send.at[2, k], wind_recv.at[2, k], device(1, 0, 0))
        for k in range(3)
    ]
    x_edges = [
        remote(
            flux_x.at[:, pl.ds(width_x - 1, 1), :],
            fx.at[levels_of(0), pl.ds(GROUP - 1, 1), :],
            edge_send.at[0, j],
            edge_recv.at[0, j],
            device(j, 1, 0),
        )
        for j in range(4)
    ]
    y_edges = [
        remote(
            fyt.at[pairs_of(0), pl.ds(GROUP + width_y - 1, 1), :],
            fyt.at[pairs_of(0), pl.ds(GROUP - 1, 1), :],
            edge_send.at[1, j],
            edge_recv.at[1, j],
            device(j, 0, 1),
        )
        for j in range(4)
    ]

    def turn_wind(j):
        first = member_of(j) * pairs

        def one_pair(k, carry):
            p = first + k
            both = fy[pl.ds(2 * p, 2)].reshape(2 * width_x, width_y)
            fyt[p, pl.ds(GROUP, width_y), :] = both.T
            return carry

        lax.fori_loop(0, pairs, one_pair, 0)

    locals_[1].wait()
    turn_wind(0)
    pl.semaphore_wait(barrier, len(partners))
    for k in range(3):
        direct[1][k].start()
        if k == 0:
            for c in x_edges:
                c.start()
            for c in halos[0][0]:
                c.start()
        direct[0][k].start()
    for c in y_edges:
        c.start()
    for j in range(1, 4):
        for c in halos[0][j]:
            c.start()

    def wait_wind(k, j):
        if j == 0:
            if k != 1:
                locals_[k].wait()
        elif j == 3:
            relay[k].wait_recv()
        else:
            direct[j - 1][k].wait_recv()

    def taps_of(read, extent, store):
        for start in [GROUP * g for g in range(extent // GROUP)] + [extent - GROUP + 1]:
            for k, w in enumerate(face_weights(read(start))):
                face[k, pl.ds(start, GROUP), :] = w

        def group(g):
            low = [face[k, pl.ds(GROUP * g, GROUP), :] for k in range(FACE)]
            high = [face[k, pl.ds(GROUP * g + 1, GROUP), :] for k in range(FACE)]
            taps = cell_taps(low, high)
            for k in range(TAPS):
                store(k, g, taps[k])
            return taps

        return group

    def sweep_x(step, j):
        field = (field0, field1)[step]
        turned = (turned0, turned1)[step]
        first = member_of(j) * pairs

        def one_pair(k, carry):
            p = first + k
            for h in range(2):
                level = 2 * p + h
                if step == 0:

                    def store(n, g, v):
                        vx[n, level, pl.ds(GROUP * g, GROUP), :] = v

                    taps_at = taps_of(lambda start: fx[level, pl.ds(GROUP - 1 + start, GROUP), :], width_x, store)
                for g in range(width_x // GROUP):
                    if step == 0:
                        taps = taps_at(g)
                    else:
                        taps = [vx[n, level, pl.ds(GROUP * g, GROUP), :] for n in range(TAPS)]
                    for t in range(trac):
                        cells = [
                            field[t, level, pl.ds(GROUP + GROUP * g + s, GROUP), :] for s in range(-RIM, RIM + 1)
                        ]
                        swept[t, pl.ds(width_x * h + GROUP * g, GROUP), :] = weighted(taps, cells)
            for t in range(trac):
                turned[t, p, pl.ds(GROUP, width_y), :] = swept[t].T
            return carry

        lax.fori_loop(0, pairs, one_pair, 0)

    def sweep_y(step, j):
        turned = (turned0, turned1)[step]
        first = member_of(j) * pairs

        def one_pair(k, carry):
            p = first + k
            if step == 0:

                def store(n, g, v):
                    vy[n, p, pl.ds(GROUP * g, GROUP), :] = v

                taps_at = taps_of(lambda start: fyt[p, pl.ds(GROUP - 1 + start, GROUP), :], width_y, store)
            for g in range(width_y // GROUP):
                if step == 0:
                    taps = taps_at(g)
                else:
                    taps = [vy[n, p, pl.ds(GROUP * g, GROUP), :] for n in range(TAPS)]
                for t in range(trac):
                    cells = [turned[t, p, pl.ds(GROUP + GROUP * g + s, GROUP), :] for s in range(-RIM, RIM + 1)]
                    swept[t, pl.ds(GROUP * g, GROUP), :] = weighted(taps, cells)
            for t in range(trac):
                mid[t, pl.ds(2 * p, 2)] = swept[t].T.reshape(2, width_x, width_y)
            return carry

        lax.fori_loop(0, pairs, one_pair, 0)

    def sweep_z(step, row):
        q = {}
        p = {}
        e = {}
        before = {}

        def cell(t, l):
            l = min(max(l, 0), levels - 1)
            if (t, l) not in q:
                q[t, l] = mid[t, l, pl.ds(row, GROUP), :]
            return q[t, l]

        def pair(t, l):
            if (t, l) not in p:
                p[t, l] = cell(t, l - 1) + cell(t, l)
            return p[t, l]

        def edge(t, l):
            if (t, l) not in e:
                e[t, l] = 8.0 * pair(t, l) - (pair(t, l - 1) + pair(t, l + 1))
            return e[t, l]

        for l in range(levels):
            if l + 1 < levels:
                coefs = coefficients(fz[l, pl.ds(row, GROUP), :])
            for t in range(trac):
                new = cell(t, l)
                if l > 0:
                    new = new + before[t]
                if l + 1 < levels:
                    positive = coefs[0]
                    o = jnp.where(positive, edge(t, l), edge(t, l + 2))
                    f = flux(coefs, edge(t, l + 1), o, jnp.where(positive, cell(t, l), cell(t, l + 1)))
                    new = new - f
                    before[t] = f
                if step == 0:
                    field1[t, l, pl.ds(GROUP + row, GROUP), :] = new
                else:
                    out[t, l, pl.ds(row, GROUP), :] = new

    def sweep_z_groups(step, start, stop):
        def one_group(g, carry):
            sweep_z(step, pl.multiple_of(g * GROUP, GROUP))
            return carry

        lax.fori_loop(start, stop, one_group, 0)

    def exchange(k):
        direct[1][k].wait_recv()
        relay[k].start()

    load.wait()
    for j in range(4):
        for c in halos[0][j]:
            c.wait_recv()
        if j == 2:
            exchange(0)
        if j != 2:
            wait_wind(0, j)
        x_edges[j].wait_recv()
        sweep_x(0, j)
        for c in packs[0][j]:
            c.start()
    for j in range(4):
        if j == 2:
            exchange(1)
        if j != 0:
            if j != 2:
                wait_wind(1, j)
            turn_wind(j)
        y_edges[j].wait_recv()
        for c in packs[0][j]:
            c.wait_recv()
        sweep_y(0, j)
    exchange(2)
    for j in (0, 1, 3):
        wait_wind(2, j)
    sweep_z(0, 0)
    sweep_z(0, width_x - GROUP)
    for j in range(4):
        for c in halos[1][j]:
            c.start()
    sweep_z_groups(0, 1, width_x // GROUP - 1)

    for j in range(4):
        for c in halos[1][j]:
            c.wait_recv()
        sweep_x(1, j)
        for c in packs[1][j]:
            c.start()
    for j in range(4):
        for c in packs[1][j]:
            c.wait_recv()
        sweep_y(1, j)
    sweep_z_groups(1, 0, width_x // GROUP)

    for step in range(2):
        for j in range(4):
            for c in halos[step][j] + packs[step][j]:
                c.wait_send()
    for c in direct[0] + direct[1] + relay + x_edges + y_edges:
        c.wait_send()


def body(sizes, tracers, flux_x, flux_y, flux_z):
    trac, levels, width_x, width_y = tracers.shape
    members = sizes[0]
    padded = pltpu.VMEM((trac, levels, width_x + 2 * GROUP, width_y), jnp.float32)
    turned = pltpu.VMEM((trac, levels // 2, width_y + 2 * GROUP, 2 * width_x), jnp.float32)
    block = pltpu.VMEM((levels, width_x, width_y), jnp.float32)
    return pl.pallas_call(
        functools.partial(kernel, sizes),
        out_shape=jax.ShapeDtypeStruct(tracers.shape, jnp.float32),
        in_specs=[pl.BlockSpec(memory_space=pltpu.HBM)] * 4,
        out_specs=pl.BlockSpec(memory_space=pltpu.VMEM),
        scratch_shapes=[
            padded,
            padded,
            turned,
            turned,
            pltpu.VMEM((trac, levels, width_x, width_y), jnp.float32),
            pltpu.VMEM((levels, width_x + GROUP, width_y), jnp.float32),
            block,
            block,
            pltpu.VMEM((levels // 2, width_y + GROUP, 2 * width_x), jnp.float32),
            pltpu.VMEM((TAPS, levels, width_x, width_y), jnp.float32),
            pltpu.VMEM((TAPS, levels // 2, width_y, 2 * width_x), jnp.float32),
            pltpu.VMEM((FACE, width_y + GROUP, LANES), jnp.float32),
            pltpu.VMEM((trac, 2 * width_x, width_y), jnp.float32),
            pltpu.SemaphoreType.DMA((4,)),
            pltpu.SemaphoreType.DMA((3, 3)),
            pltpu.SemaphoreType.DMA((3, 3)),
            pltpu.SemaphoreType.DMA((2, 4)),
            pltpu.SemaphoreType.DMA((2, 4)),
            pltpu.SemaphoreType.DMA((2, 4, 2)),
            pltpu.SemaphoreType.DMA((2, 4, 2)),
            pltpu.SemaphoreType.DMA((2, 4, 2)),
            pltpu.SemaphoreType.DMA((2, 4, 2)),
        ],
        compiler_params=pltpu.CompilerParams(
            collective_id=0, has_side_effects=True
        ),
    )(tracers, flux_x, flux_y, flux_z)


def solution(mesh):
    sizes = (mesh.shape["member"], mesh.shape["gx"], mesh.shape["gy"])
    return jax.shard_map(
        functools.partial(body, sizes),
        mesh=mesh,
        in_specs=(
            P("member", None, "gx", "gy"),
            P("member", "gx", "gy"),
            P("member", "gx", "gy"),
            P("member", "gx", "gy"),
        ),
        out_specs=P("member", None, "gx", "gy"),
        check_vma=False,
    )
```

```python
import functools

import jax
import jax.numpy as jnp
from jax import lax
from jax.experimental import pallas as pl
from jax.experimental.pallas import tpu as pltpu
from jax.sharding import PartitionSpec as P

MESH = pl.DeviceIdType.MESH
LANES = 128
GROUP = 8
RIM = 3
TAPS = 2 * RIM + 1
FACE = 2 * RIM


def coefficients(c):
    s = jnp.abs(c)
    t = 1.0 - s
    ct = c * t * (1.0 / 12.0)
    return c > 0, ct * t, ct * s, c * s * (3.0 - 2.0 * s)


def flux(coefs, e, o, upwind):
    _, near, far, mean = coefs
    return near * e - far * o + mean * upwind


def face_weights(c):
    positive, near, far, mean = coefficients(c)
    near7 = 7.0 * near
    far7 = 7.0 * far
    second = -(near + far7)
    upwind = near7 - far7 + mean
    downwind = near7 + far
    last = -near
    zero = jnp.zeros_like(c)
    return (
        jnp.where(positive, far, zero),
        jnp.where(positive, second, last),
        jnp.where(positive, upwind, downwind),
        jnp.where(positive, downwind, upwind),
        jnp.where(positive, last, second),
        jnp.where(positive, zero, far),
    )


def cell_taps(low, high):
    taps = [low[0]]
    for k in range(1, FACE):
        taps.append(low[k] - high[k - 1])
    taps.append(-high[FACE - 1])
    taps[RIM] = taps[RIM] + 1.0
    return taps


def weighted(taps, cells):
    terms = [a * b for a, b in zip(taps, cells)]
    while len(terms) > 1:
        terms = [sum(terms[i : i + 2]) if i + 1 < len(terms) else terms[i] for i in range(0, len(terms), 2)]
    return terms[0]


def kernel(
    sizes,
    tracers,
    flux_x,
    flux_y,
    flux_z,
    out,
    field0,
    field1,
    turned0,
    turned1,
    mid,
    fx,
    fy,
    fz,
    fyt,
    vx,
    vy,
    face,
    swept,
    local_sem,
    wind_send,
    wind_recv,
    edge_send,
    edge_recv,
    halo_send,
    halo_recv,
    pack_send,
    pack_recv,
    out_sem,
    far,
    known,
):
    members, n_x, n_y = sizes
    trac, levels, width_x, width_y = tracers.shape
    slab = levels // members
    pairs = slab // 2
    m = lax.axis_index("member")
    ix = lax.axis_index("gx")
    iy = lax.axis_index("gy")

    def member_of(j):
        if j == 0:
            return m
        if j == 1:
            return m + 1 - 2 * lax.rem(m, 2)
        if j == 2:
            return lax.rem(m + 2, 4)
        return 3 - m

    def device(j, dx, dy):
        return (member_of(j), lax.rem(ix + dx + n_x, n_x), lax.rem(iy + dy + n_y, n_y))

    last = n_y - 1
    barrier = pltpu.get_barrier_semaphore()
    x_steps = (1,) if n_x == 2 else (1, -1)
    near = [(1, 0, 0), (2, 0, 0), (3, 0, 0)] + [(0, d, 0) for d in x_steps]
    up = (0, 0, 1)
    down = (0, 0, -1)

    def signal(semaphore, partner):
        pl.semaphore_signal(semaphore, inc=1, device_id=device(*partner), device_id_type=MESH)

    for partner in near:
        signal(barrier, partner)
    pl.when(iy < last)(lambda: signal(barrier, up))
    pl.when(iy > 0)(lambda: signal(barrier, down))

    def levels_of(j):
        return pl.ds(member_of(j) * slab, slab)

    def pairs_of(j):
        return pl.ds(member_of(j) * pairs, pairs)

    inner = pl.ds(GROUP, width_x)
    every = (0, width_x)
    parts = (
        (flux_x, fx, GROUP, every),
        (flux_y, fy, 0, every),
        (flux_z, fz, 0, (0, GROUP)),
        (flux_z, fz, 0, (width_x - GROUP, GROUP)),
        (flux_z, fz, 0, (GROUP, width_x - 2 * GROUP)),
    )

    def wind_src(k):
        start, size = parts[k][3]
        return parts[k][0].at[:, pl.ds(start, size), :]

    def wind_dst(k, j):
        _, block, offset, (start, size) = parts[k]
        return block.at[levels_of(j), pl.ds(offset + start, size), :]

    locals_ = [
        pltpu.make_async_copy(flux_x, fx.at[levels_of(0), inner, :], local_sem.at[0]),
        pltpu.make_async_copy(flux_y, fy.at[levels_of(0)], local_sem.at[1]),
        pltpu.make_async_copy(flux_z, fz.at[levels_of(0)], local_sem.at[2]),
    ]
    load = pltpu.make_async_copy(tracers, field0.at[:, :, inner, :], local_sem.at[3])
    locals_[1].start()
    locals_[0].start()
    load.start()
    locals_[2].start()

    def remote(src, dst, send, recv, dev):
        return pltpu.make_async_remote_copy(
            src_ref=src, dst_ref=dst, send_sem=send, recv_sem=recv, device_id=dev, device_id_type=MESH
        )

    def halo_copies(step, j):
        target = (field0, field1)[step]
        ls = levels_of(j)
        if step == 0:
            low_src = tracers.at[:, ls, pl.ds(0, RIM), :]
            high_src = tracers.at[:, ls, pl.ds(width_x - RIM, RIM), :]
        else:
            low_src = field1.at[:, ls, pl.ds(GROUP, RIM), :]
            high_src = field1.at[:, ls, pl.ds(GROUP + width_x - RIM, RIM), :]
        return (
            remote(
                high_src,
                target.at[:, ls, pl.ds(GROUP - RIM, RIM), :],
                halo_send.at[step, j, 0],
                halo_recv.at[step, j, 0],
                device(0, 1, 0),
            ),
            remote(
                low_src,
                target.at[:, ls, pl.ds(width_x + GROUP, RIM), :],
                halo_send.at[step, j, 1],
                halo_recv.at[step, j, 1],
                device(0, -1, 0),
            ),
        )

    def pack_copies(step, j):
        turned = (turned0, turned1)[step]
        ps = pairs_of(j)
        return (
            remote(
                turned.at[:, ps, pl.ds(GROUP + width_y - RIM, RIM), :],
                turned.at[:, ps, pl.ds(GROUP - RIM, RIM), :],
                pack_send.at[step, j, 0],
                pack_recv.at[step, j, 0],
                device(0, 0, 1),
            ),
            remote(
                turned.at[:, ps, pl.ds(GROUP, RIM), :],
                turned.at[:, ps, pl.ds(GROUP + width_y, RIM), :],
                pack_send.at[step, j, 1],
                pack_recv.at[step, j, 1],
                device(0, 0, -1),
            ),
        )

    halos = [[halo_copies(step, j) for j in range(4)] for step in range(2)]
    packs = [[pack_copies(step, j) for j in range(4)] for step in range(2)]
    direct = [
        [
            remote(wind_src(k), wind_dst(k, 0), wind_send.at[j - 1, k], wind_recv.at[j - 1, k], device(j, 0, 0))
            for k in range(len(parts))
        ]
        for j in (1, 2)
    ]
    relay = [
        remote(wind_dst(k, 2), wind_dst(k, 2), wind_send.at[2, k], wind_recv.at[2, k], device(1, 0, 0))
        for k in range(len(parts))
    ]

    x_edges = [
        remote(
            flux_x.at[:, pl.ds(width_x - 1, 1), :],
            fx.at[levels_of(0), pl.ds(GROUP - 1, 1), :],
            edge_send.at[0, j],
            edge_recv.at[0, j],
            device(j, 1, 0),
        )
        for j in range(4)
    ]
    y_edges = [
        remote(
            fyt.at[pairs_of(0), pl.ds(GROUP + width_y - 1, 1), :],
            fyt.at[pairs_of(0), pl.ds(GROUP - 1, 1), :],
            edge_send.at[1, j],
            edge_recv.at[1, j],
            device(j, 0, 1),
        )
        for j in range(4)
    ]

    def turn_wind(j):
        first = member_of(j) * pairs

        def one_pair(k, carry):
            p = first + k
            both = fy[pl.ds(2 * p, 2)].reshape(2 * width_x, width_y)
            fyt[p, pl.ds(GROUP, width_y), :] = both.T
            return carry

        lax.fori_loop(0, pairs, one_pair, 0)

    locals_[1].wait()
    turn_wind(0)
    pl.semaphore_wait(barrier, len(near) + lax.min(iy, 1) + lax.min(last - iy, 1))
    signal(known.at[0], (0, -1, 0))
    pl.when(iy > 0)(lambda: signal(known.at[1], down))
    pl.when(iy == 0)(lambda: signal(far.at[1], up))
    pl.when(iy == last - 1)(lambda: signal(far.at[0], down))
    direct[1][0].start()
    x_edges[0].start()
    for c in halos[0][0]:
        c.start()
    direct[0][0].start()
    for j in range(1, 4):
        for c in halos[0][j]:
            c.start()

    pl.semaphore_wait(known.at[0], 1)
    for c in x_edges[1:]:
        c.start()

    @pl.when(iy < last)
    def _():
        pl.semaphore_wait(known.at[1], 1)
        for c in y_edges:
            c.start()

    direct[1][1].start()
    direct[0][1].start()

    @pl.when((iy > 0) & (iy < last - 1))
    def _():
        pl.semaphore_wait(far.at[0], 1)
        signal(far.at[0], down)

    @pl.when((iy > 0) & (iy < last))
    def _():
        pl.semaphore_wait(far.at[1], 1)
        signal(far.at[1], up)

    def ends_are_in():
        @pl.when(iy == 0)
        def _():
            pl.semaphore_wait(far.at[0], 1)

        @pl.when(iy == last)
        def _():
            pl.semaphore_wait(far.at[1], 1)
            for c in y_edges:
                c.start()

    def wait_wind(k, j):
        if j == 3:
            relay[k].wait_recv()
        else:
            direct[j - 1][k].wait_recv()

    def taps_of(read, extent, store):
        for start in [GROUP * g for g in range(extent // GROUP)] + [extent - GROUP + 1]:
            for k, w in enumerate(face_weights(read(start))):
                face[k, pl.ds(start, GROUP), :] = w

        def group(g):
            low = [face[k, pl.ds(GROUP * g, GROUP), :] for k in range(FACE)]
            high = [face[k, pl.ds(GROUP * g + 1, GROUP), :] for k in range(FACE)]
            taps = cell_taps(low, high)
            for k in range(TAPS):
                store(k, g, taps[k])
            return taps

        return group

    def sweep_x(step, j):
        field = (field0, field1)[step]
        turned = (turned0, turned1)[step]
        first = member_of(j) * pairs

        def one_pair(k, carry):
            p = first + k
            for h in range(2):
                level = 2 * p + h
                if step == 0:

                    def store(n, g, v):
                        vx[n, level, pl.ds(GROUP * g, GROUP), :] = v

                    taps_at = taps_of(lambda start: fx[level, pl.ds(GROUP - 1 + start, GROUP), :], width_x, store)
                for g in range(width_x // GROUP):
                    if step == 0:
                        taps = taps_at(g)
                    else:
                        taps = [vx[n, level, pl.ds(GROUP * g, GROUP), :] for n in range(TAPS)]
                    for t in range(trac):
                        cells = [
                            field[t, level, pl.ds(GROUP + GROUP * g + s, GROUP), :] for s in range(-RIM, RIM + 1)
                        ]
                        swept[t, pl.ds(width_x * h + GROUP * g, GROUP), :] = weighted(taps, cells)
            for t in range(trac):
                turned[t, p, pl.ds(GROUP, width_y), :] = swept[t].T
            return carry

        lax.fori_loop(0, pairs, one_pair, 0)

    def sweep_y(step, j):
        turned = (turned0, turned1)[step]
        first = member_of(j) * pairs

        def one_pair(k, carry):
            p = first + k
            if step == 0:

                def store(n, g, v):
                    vy[n, p, pl.ds(GROUP * g, GROUP), :] = v

                taps_at = taps_of(lambda start: fyt[p, pl.ds(GROUP - 1 + start, GROUP), :], width_y, store)
            for g in range(width_y // GROUP):
                if step == 0:
                    taps = taps_at(g)
                else:
                    taps = [vy[n, p, pl.ds(GROUP * g, GROUP), :] for n in range(TAPS)]
                for t in range(trac):
                    cells = [turned[t, p, pl.ds(GROUP + GROUP * g + s, GROUP), :] for s in range(-RIM, RIM + 1)]
                    swept[t, pl.ds(GROUP * g, GROUP), :] = weighted(taps, cells)
            for t in range(trac):
                mid[t, pl.ds(2 * p, 2)] = swept[t].T.reshape(2, width_x, width_y)
            return carry

        lax.fori_loop(0, pairs, one_pair, 0)

    def sweep_z(step, row):
        q = {}
        p = {}
        e = {}
        before = {}

        def cell(t, l):
            l = min(max(l, 0), levels - 1)
            if (t, l) not in q:
                q[t, l] = mid[t, l, pl.ds(row, GROUP), :]
            return q[t, l]

        def pair(t, l):
            if (t, l) not in p:
                p[t, l] = cell(t, l - 1) + cell(t, l)
            return p[t, l]

        def edge(t, l):
            if (t, l) not in e:
                e[t, l] = 8.0 * pair(t, l) - (pair(t, l - 1) + pair(t, l + 1))
            return e[t, l]

        for l in range(levels):
            if l + 1 < levels:
                coefs = coefficients(fz[l, pl.ds(row, GROUP), :])
            for t in range(trac):
                new = cell(t, l)
                if l > 0:
                    new = new + before[t]
                if l + 1 < levels:
                    positive = coefs[0]
                    o = jnp.where(positive, edge(t, l), edge(t, l + 2))
                    f = flux(coefs, edge(t, l + 1), o, jnp.where(positive, cell(t, l), cell(t, l + 1)))
                    new = new - f
                    before[t] = f
                (field1, field0)[step][t, l, pl.ds(GROUP + row, GROUP), :] = new

    def sweep_z_groups(step, start, stop):
        def one_group(g, carry):
            sweep_z(step, pl.multiple_of(g * GROUP, GROUP))
            return carry

        lax.fori_loop(start, stop, one_group, 0)

    def exchange(k):
        direct[1][k].wait_recv()
        relay[k].start()

    def store(row):
        group = row // GROUP
        return pltpu.make_async_copy(
            field0.at[:, :, pl.ds(GROUP + row, GROUP), :], out.at[:, :, pl.ds(row, GROUP), :], out_sem.at[group]
        )

    locals_[0].wait()
    load.wait()
    for j in range(4):
        for c in halos[0][j]:
            c.wait_recv()
        if j == 2:
            exchange(0)
        elif j > 0:
            wait_wind(0, j)
        x_edges[j].wait_recv()
        sweep_x(0, j)
        if j == 0:
            ends_are_in()
            for k in range(2, len(parts)):
                direct[1][k].start()
                direct[0][k].start()
        for c in packs[0][j]:
            c.start()
    for j in range(4):
        if j == 2:
            exchange(1)
        if j == 3:
            exchange(2)
            exchange(3)
        if j > 0:
            if j != 2:
                wait_wind(1, j)
            turn_wind(j)
        y_edges[j].wait_recv()
        for c in packs[0][j]:
            c.wait_recv()
        sweep_y(0, j)
    locals_[2].wait()
    for k in (2, 3):
        for j in (1, 3):
            wait_wind(k, j)
    sweep_z(0, 0)
    sweep_z(0, width_x - GROUP)
    for j in range(4):
        for c in halos[1][j]:
            c.start()
    exchange(4)
    for j in (1, 3):
        wait_wind(4, j)
    sweep_z_groups(0, 1, width_x // GROUP - 1)

    for j in range(4):
        for c in halos[1][j]:
            c.wait_recv()
        sweep_x(1, j)
        for c in packs[1][j]:
            c.start()
    for j in range(4):
        for c in packs[1][j]:
            c.wait_recv()
        sweep_y(1, j)

    def last_group(g, carry):
        row = pl.multiple_of(g * GROUP, GROUP)
        sweep_z(1, row)
        store(row).start()
        return carry

    lax.fori_loop(0, width_x // GROUP, last_group, 0)
    for g in range(width_x // GROUP):
        store(g * GROUP).wait()

    for step in range(2):
        for j in range(4):
            for c in halos[step][j] + packs[step][j]:
                c.wait_send()
    for c in direct[0] + direct[1] + relay + x_edges + y_edges:
        c.wait_send()


def body(sizes, tracers, flux_x, flux_y, flux_z):
    trac, levels, width_x, width_y = tracers.shape
    members = sizes[0]
    padded = pltpu.VMEM((trac, levels, width_x + 2 * GROUP, width_y), jnp.float32)
    turned = pltpu.VMEM((trac, levels // 2, width_y + 2 * GROUP, 2 * width_x), jnp.float32)
    block = pltpu.VMEM((levels, width_x, width_y), jnp.float32)
    return pl.pallas_call(
        functools.partial(kernel, sizes),
        out_shape=jax.ShapeDtypeStruct(tracers.shape, jnp.float32),
        in_specs=[pl.BlockSpec(memory_space=pltpu.HBM)] * 4,
        out_specs=pl.BlockSpec(memory_space=pltpu.HBM),
        scratch_shapes=[
            padded,
            padded,
            turned,
            turned,
            pltpu.VMEM((trac, levels, width_x, width_y), jnp.float32),
            pltpu.VMEM((levels, width_x + GROUP, width_y), jnp.float32),
            block,
            block,
            pltpu.VMEM((levels // 2, width_y + GROUP, 2 * width_x), jnp.float32),
            pltpu.VMEM((TAPS, levels, width_x, width_y), jnp.float32),
            pltpu.VMEM((TAPS, levels // 2, width_y, 2 * width_x), jnp.float32),
            pltpu.VMEM((FACE, width_y + GROUP, LANES), jnp.float32),
            pltpu.VMEM((trac, 2 * width_x, width_y), jnp.float32),
            pltpu.SemaphoreType.DMA((4,)),
            pltpu.SemaphoreType.DMA((3, 5)),
            pltpu.SemaphoreType.DMA((3, 5)),
            pltpu.SemaphoreType.DMA((2, 4)),
            pltpu.SemaphoreType.DMA((2, 4)),
            pltpu.SemaphoreType.DMA((2, 4, 2)),
            pltpu.SemaphoreType.DMA((2, 4, 2)),
            pltpu.SemaphoreType.DMA((2, 4, 2)),
            pltpu.SemaphoreType.DMA((2, 4, 2)),
            pltpu.SemaphoreType.DMA((width_x // GROUP,)),
            pltpu.SemaphoreType.REGULAR((2,)),
            pltpu.SemaphoreType.REGULAR((2,)),
        ],
        compiler_params=pltpu.CompilerParams(
            collective_id=0, has_side_effects=True
        ),
    )(tracers, flux_x, flux_y, flux_z)


def solution(mesh):
    sizes = (mesh.shape["member"], mesh.shape["gx"], mesh.shape["gy"])
    return jax.shard_map(
        functools.partial(body, sizes),
        mesh=mesh,
        in_specs=(
            P("member", None, "gx", "gy"),
            P("member", "gx", "gy"),
            P("member", "gx", "gy"),
            P("member", "gx", "gy"),
        ),
        out_specs=P("member", None, "gx", "gy"),
        check_vma=False,
    )
```

```python
import functools

import jax
import jax.numpy as jnp
from jax import lax
from jax.experimental import pallas as pl
from jax.experimental.pallas import tpu as pltpu
from jax.sharding import PartitionSpec as P

MESH = pl.DeviceIdType.MESH
LANES = 128
GROUP = 8
RIM = 3
TAPS = 2 * RIM + 1
FACE = 2 * RIM


def coefficients(c):
    s = jnp.abs(c)
    t = 1.0 - s
    ct = c * t * (1.0 / 12.0)
    return c > 0, ct * t, ct * s, c * s * (3.0 - 2.0 * s)


def flux(coefs, e, o, upwind):
    _, near, far, mean = coefs
    return near * e - far * o + mean * upwind


def face_weights(c):
    positive, near, far, mean = coefficients(c)
    near7 = 7.0 * near
    far7 = 7.0 * far
    second = -(near + far7)
    upwind = near7 - far7 + mean
    downwind = near7 + far
    last = -near
    zero = jnp.zeros_like(c)
    return (
        jnp.where(positive, far, zero),
        jnp.where(positive, second, last),
        jnp.where(positive, upwind, downwind),
        jnp.where(positive, downwind, upwind),
        jnp.where(positive, last, second),
        jnp.where(positive, zero, far),
    )


def cell_taps(low, high):
    taps = [low[0]]
    for k in range(1, FACE):
        taps.append(low[k] - high[k - 1])
    taps.append(-high[FACE - 1])
    taps[RIM] = taps[RIM] + 1.0
    return taps


def weighted(taps, cells):
    terms = [a * b for a, b in zip(taps, cells)]
    while len(terms) > 1:
        terms = [sum(terms[i : i + 2]) if i + 1 < len(terms) else terms[i] for i in range(0, len(terms), 2)]
    return terms[0]


def column_sweep(field, winds, row, put):
    trac, levels = field.shape[0], field.shape[1]
    q = {}
    p = {}
    e = {}
    before = {}

    def cell(t, l):
        l = min(max(l, 0), levels - 1)
        if (t, l) not in q:
            q[t, l] = field[t, l, pl.ds(row, GROUP), :]
        return q[t, l]

    def pair(t, l):
        if (t, l) not in p:
            p[t, l] = cell(t, l - 1) + cell(t, l)
        return p[t, l]

    def edge(t, l):
        if (t, l) not in e:
            e[t, l] = 8.0 * pair(t, l) - (pair(t, l - 1) + pair(t, l + 1))
        return e[t, l]

    for l in range(levels):
        if l + 1 < levels:
            coefs = coefficients(winds[l, pl.ds(row, GROUP), :])
        for t in range(trac):
            new = cell(t, l)
            if l > 0:
                new = new + before[t]
            if l + 1 < levels:
                positive = coefs[0]
                o = jnp.where(positive, edge(t, l), edge(t, l + 2))
                f = flux(coefs, edge(t, l + 1), o, jnp.where(positive, cell(t, l), cell(t, l + 1)))
                new = new - f
                before[t] = f
            put(t, l, new)


def last_kernel(field, winds, out, staged, out_sem):
    def store(row):
        rows = pl.ds(row, GROUP)
        return pltpu.make_async_copy(staged.at[:, :, rows, :], out.at[:, :, rows, :], out_sem.at[row // GROUP])

    def one_group(g, carry):
        row = pl.multiple_of(g * GROUP, GROUP)

        def put(t, l, new):
            staged[t, l, pl.ds(row, GROUP), :] = new

        column_sweep(field, winds, row, put)
        store(row).start()
        return carry

    groups = field.shape[2] // GROUP
    lax.fori_loop(0, groups, one_group, 0)
    for g in range(groups):
        store(g * GROUP).wait()


def kernel(
    sizes,
    tracers,
    flux_x,
    flux_y,
    flux_z,
    field_out,
    winds_out,
    field0,
    field1,
    turned0,
    turned1,
    mid,
    fx,
    fy,
    fz,
    fyt,
    vx,
    vy,
    face,
    swept,
    rim_before,
    rim_after,
    rim_flux,
    far_flux,
    far_rim,
    corner,
    far_corner,
    far_taps,
    rim_winds,
    local_sem,
    wind_send,
    wind_recv,
    edge_send,
    edge_recv,
    halo_send,
    halo_recv,
    pack_send,
    pack_recv,
    out_sem,
    far,
    known,
    rim_send,
    rim_recv,
):
    members, n_x, n_y = sizes
    trac, levels, width_x, width_y = tracers.shape
    slab = levels // members
    pairs = slab // 2
    m = lax.axis_index("member")
    ix = lax.axis_index("gx")
    iy = lax.axis_index("gy")

    def member_of(j):
        if j == 0:
            return m
        if j == 1:
            return m + 1 - 2 * lax.rem(m, 2)
        if j == 2:
            return lax.rem(m + 2, 4)
        return 3 - m

    def device(j, dx, dy):
        return (member_of(j), lax.rem(ix + dx + n_x, n_x), lax.rem(iy + dy + n_y, n_y))

    last = n_y - 1
    barrier = pltpu.get_barrier_semaphore()
    x_steps = (1,) if n_x == 2 else (1, -1)
    near = [(1, 0, 0), (2, 0, 0), (3, 0, 0)] + [(0, d, 0) for d in x_steps]
    up = (0, 0, 1)
    down = (0, 0, -1)

    def signal(semaphore, partner):
        pl.semaphore_signal(semaphore, inc=1, device_id=device(*partner), device_id_type=MESH)

    for partner in near:
        signal(barrier, partner)
    pl.when(iy < last)(lambda: signal(barrier, up))
    pl.when(iy > 0)(lambda: signal(barrier, down))

    def levels_of(j):
        return pl.ds(member_of(j) * slab, slab)

    def pairs_of(j):
        return pl.ds(member_of(j) * pairs, pairs)

    inner = pl.ds(GROUP, width_x)
    every = (0, width_x)
    parts = (
        (flux_x, fx, GROUP, every),
        (flux_y, fy, 0, every),
        (flux_z, fz, 0, (0, GROUP)),
        (flux_z, fz, 0, (width_x - GROUP, GROUP)),
        (flux_z, fz, 0, (GROUP, width_x - 2 * GROUP)),
    )

    def wind_src(k):
        start, size = parts[k][3]
        return parts[k][0].at[:, pl.ds(start, size), :]

    def wind_dst(k, j):
        _, block, offset, (start, size) = parts[k]
        return block.at[levels_of(j), pl.ds(offset + start, size), :]

    locals_ = [
        pltpu.make_async_copy(flux_x, fx.at[levels_of(0), inner, :], local_sem.at[0]),
        pltpu.make_async_copy(flux_y, fy.at[levels_of(0)], local_sem.at[1]),
        pltpu.make_async_copy(flux_z, fz.at[levels_of(0)], local_sem.at[2]),
    ]
    load = pltpu.make_async_copy(tracers, field0.at[:, :, inner, :], local_sem.at[3])
    locals_[1].start()
    locals_[0].start()
    load.start()
    locals_[2].start()

    def remote(src, dst, send, recv, dev):
        return pltpu.make_async_remote_copy(
            src_ref=src, dst_ref=dst, send_sem=send, recv_sem=recv, device_id=dev, device_id_type=MESH
        )

    def halo_copies(step, j):
        target = (field0, field1)[step]
        ls = levels_of(j)
        if step == 0:
            low_src = tracers.at[:, ls, pl.ds(0, RIM), :]
            high_src = tracers.at[:, ls, pl.ds(width_x - RIM, RIM), :]
        else:
            low_src = field1.at[:, ls, pl.ds(GROUP, RIM), :]
            high_src = field1.at[:, ls, pl.ds(GROUP + width_x - RIM, RIM), :]
        return (
            remote(
                high_src,
                target.at[:, ls, pl.ds(GROUP - RIM, RIM), :],
                halo_send.at[step, j, 0],
                halo_recv.at[step, j, 0],
                device(0, 1, 0),
            ),
            remote(
                low_src,
                target.at[:, ls, pl.ds(width_x + GROUP, RIM), :],
                halo_send.at[step, j, 1],
                halo_recv.at[step, j, 1],
                device(0, -1, 0),
            ),
        )

    def pack_copies(step, j):
        turned = (turned0, turned1)[step]
        ps = pairs_of(j)
        return (
            remote(
                turned.at[:, ps, pl.ds(GROUP + width_y - RIM, RIM), :],
                turned.at[:, ps, pl.ds(GROUP - RIM, RIM), :],
                pack_send.at[step, j, 0],
                pack_recv.at[step, j, 0],
                device(0, 0, 1),
            ),
            remote(
                turned.at[:, ps, pl.ds(GROUP, RIM), :],
                turned.at[:, ps, pl.ds(GROUP + width_y, RIM), :],
                pack_send.at[step, j, 1],
                pack_recv.at[step, j, 1],
                device(0, 0, -1),
            ),
        )

    halos = [[halo_copies(step, j) for j in range(4)] for step in range(2)]
    packs = [[pack_copies(0, j) for j in range(4)], [() for j in range(4)]]
    above = pl.ds(0, RIM)
    below = pl.ds(GROUP - RIM, RIM)

    def rim_pair(src, dst, n, dx):
        return [
            remote(
                src.at[..., rows, :], dst.at[..., rows, :], rim_send.at[n + i], rim_recv.at[n + i], device(0, dx, dy)
            )
            for i, (rows, dy) in enumerate(((below, 1), (above, -1)))
        ]

    flux_sends = rim_pair(rim_flux, far_flux, 0, 0)
    rim_sends = rim_pair(rim_after, far_rim, 2, 0) + rim_pair(corner, far_corner.at[0], 4, 1)
    if n_x > 2:
        rim_sends += rim_pair(corner, far_corner.at[1], 6, -1)

    lane = lax.broadcasted_iota(jnp.int32, (GROUP, LANES), 1)
    first_half = lane < width_x
    across = lax.rem(lane, width_x)
    slot = lax.rem(lane + LANES - (width_x - RIM), width_x)
    upper_rows = lax.broadcasted_iota(jnp.int32, (GROUP, LANES), 0) < GROUP // 2
    n_pairs = levels // 2
    y_groups = tuple(range(width_y // GROUP))

    def rim_of(tile):
        return jnp.where(upper_rows, tile[:GROUP], tile[width_y - GROUP :])

    def turn_flux_rims():
        def one_pair(p, carry):
            for u in range(2):
                both = fx[pl.ds(2 * p, 2), pl.ds(GROUP - 1 + u, width_x), :]
                rim_flux[u, p] = rim_of(both.reshape(2 * width_x, width_y).T)
            return carry

        lax.fori_loop(0, n_pairs, one_pair, 0)

    def rim_taps():
        for p in range(n_pairs):
            taps = cell_taps(face_weights(far_flux[0, p]), face_weights(far_flux[1, p]))
            for k in range(TAPS):
                far_taps[k, p] = taps[k]

    def turn_wind_rims(j):
        for n in range(pairs):
            p = member_of(j) * pairs + n
            rim_winds[p] = rim_of(fz[pl.ds(2 * p, 2)].reshape(2 * width_x, width_y).T)

    def rim_sweep_z():
        winds_at = [rim_winds[p] for p in range(n_pairs)]
        winds_at[-1] = jnp.where(first_half, winds_at[-1], 0.0)

        def swap(x):
            return pltpu.roll(x, width_x, 1)

        for t in range(trac):
            q = [rim_before[t, p] for p in range(n_pairs)]
            r = [swap(x) for x in q]
            top = jnp.where(first_half, q[0], r[0])
            bottom = jnp.where(first_half, r[-1], q[-1])

            def at(rows, p):
                return top if p < 0 else bottom if p >= n_pairs else rows[p]

            def next_level(p):
                return jnp.where(first_half, at(r, p), at(r, p + 1))

            flows = []
            for p in range(n_pairs):
                cells = [
                    at(q, p - 1),
                    jnp.where(first_half, at(r, p - 1), r[p]),
                    q[p],
                    next_level(p),
                    at(q, p + 1),
                    next_level(p + 1),
                ]
                flows.append(weighted(face_weights(winds_at[p]), cells))
            turned_flows = [swap(f) for f in flows]
            packed = None
            for p in range(n_pairs):
                earlier = turned_flows[p - 1] if p else jnp.zeros_like(top)
                new = q[p] + (jnp.where(first_half, earlier, turned_flows[p]) - flows[p])
                rim_after[t, p] = new
                moved = pltpu.roll(new, GROUP * p, 1) if p else new
                packed = moved if packed is None else jnp.where(slot // GROUP == p, moved, packed)
            corner[t] = packed

    def rim_sweep_x():
        for t in range(trac):
            beyond = far_corner[0, t]
            if n_x > 2:
                beyond = jnp.where(lax.rem(slot, GROUP) < RIM, beyond, far_corner[1, t])
            for p in range(n_pairs):
                own = far_rim[t, p]
                other = pltpu.roll(beyond, (width_x - GROUP * p) % LANES, 1)
                cells = []
                for d in range(-RIM, RIM + 1):
                    if d == 0:
                        cells.append(own)
                        continue
                    inside = (across + d >= 0) & (across + d < width_x)
                    cells.append(
                        jnp.where(inside, pltpu.roll(own, -d % LANES, 1), pltpu.roll(other, -d % LANES, 1))
                    )
                new = weighted([far_taps[k, p] for k in range(TAPS)], cells)
                turned1[t, p, pl.ds(GROUP - RIM, RIM), :] = new[GROUP - RIM :]
                turned1[t, p, pl.ds(GROUP + width_y, RIM), :] = new[:RIM]

    direct = [
        [
            remote(wind_src(k), wind_dst(k, 0), wind_send.at[j - 1, k], wind_recv.at[j - 1, k], device(j, 0, 0))
            for k in range(len(parts))
        ]
        for j in (1, 2)
    ]
    relay = [
        remote(wind_dst(k, 2), wind_dst(k, 2), wind_send.at[2, k], wind_recv.at[2, k], device(1, 0, 0))
        for k in range(len(parts))
    ]

    x_edges = [
        remote(
            flux_x.at[:, pl.ds(width_x - 1, 1), :],
            fx.at[levels_of(0), pl.ds(GROUP - 1, 1), :],
            edge_send.at[0, j],
            edge_recv.at[0, j],
            device(j, 1, 0),
        )
        for j in range(4)
    ]
    y_edges = [
        remote(
            fyt.at[pairs_of(0), pl.ds(GROUP + width_y - 1, 1), :],
            fyt.at[pairs_of(0), pl.ds(GROUP - 1, 1), :],
            edge_send.at[1, j],
            edge_recv.at[1, j],
            device(j, 0, 1),
        )
        for j in range(4)
    ]

    def turn_wind(j):
        first = member_of(j) * pairs

        def one_pair(k, carry):
            p = first + k
            both = fy[pl.ds(2 * p, 2)].reshape(2 * width_x, width_y)
            fyt[p, pl.ds(GROUP, width_y), :] = both.T
            return carry

        lax.fori_loop(0, pairs, one_pair, 0)

    def put_faces(read, start, row):
        for k, w in enumerate(face_weights(read(start))):
            face[k, pl.ds(row, GROUP), :] = w

    def put_taps(store, g, row):
        low = [face[k, pl.ds(row, GROUP), :] for k in range(FACE)]
        high = [face[k, pl.ds(row + 1, GROUP), :] for k in range(FACE)]
        for k, tap in enumerate(cell_taps(low, high)):
            store(k, g, tap)

    def inner_taps(read, store, extent):
        for g in range(extent // GROUP):
            put_faces(read, GROUP * g + 1, GROUP * g + GROUP)
        for g in range(1, extent // GROUP):
            put_taps(store, g, GROUP * g + GROUP - 1)

    def first_taps(read, store):
        put_faces(read, 0, 0)
        put_faces(read, 1, 1)
        put_taps(store, 0, 0)

    def x_taps(j, inside):
        first = member_of(j) * slab

        def one_level(n, carry):
            level = first + n

            def read(start):
                return fx[level, pl.ds(GROUP - 1 + start, GROUP), :]

            def store(k, g, tap):
                vx[k, level, pl.ds(GROUP * g, GROUP), :] = tap

            if inside:
                inner_taps(read, store, width_x)
            else:
                first_taps(read, store)
            return carry

        lax.fori_loop(0, slab, one_level, 0)

    def y_taps(j, inside):
        first = member_of(j) * pairs

        def one_pair(n, carry):
            p = first + n

            def read(start):
                return fyt[p, pl.ds(GROUP - 1 + start, GROUP), :]

            def store(k, g, tap):
                vy[k, p, pl.ds(GROUP * g, GROUP), :] = tap

            if inside:
                inner_taps(read, store, width_y)
            else:
                first_taps(read, store)
            return carry

        lax.fori_loop(0, pairs, one_pair, 0)

    locals_[1].wait()
    turn_wind(0)
    pl.semaphore_wait(barrier, len(near) + lax.min(iy, 1) + lax.min(last - iy, 1))
    signal(known.at[0], (0, -1, 0))
    pl.when(iy > 0)(lambda: signal(known.at[1], down))
    pl.when(iy == 0)(lambda: signal(far.at[1], up))
    pl.when(iy == last - 1)(lambda: signal(far.at[0], down))
    direct[1][0].start()
    x_edges[0].start()
    for c in halos[0][0]:
        c.start()
    direct[0][0].start()
    for j in range(1, 4):
        for c in halos[0][j]:
            c.start()

    locals_[0].wait()
    x_taps(0, True)
    y_taps(0, True)

    pl.semaphore_wait(known.at[0], 1)
    for c in x_edges[1:]:
        c.start()

    @pl.when(iy < last)
    def _():
        pl.semaphore_wait(known.at[1], 1)
        for c in y_edges:
            c.start()

    direct[1][1].start()
    direct[0][1].start()

    @pl.when((iy > 0) & (iy < last - 1))
    def _():
        pl.semaphore_wait(far.at[0], 1)
        signal(far.at[0], down)

    @pl.when((iy > 0) & (iy < last))
    def _():
        pl.semaphore_wait(far.at[1], 1)
        signal(far.at[1], up)

    def ends_are_in():
        @pl.when(iy == 0)
        def _():
            pl.semaphore_wait(far.at[0], 1)

        @pl.when(iy == last)
        def _():
            pl.semaphore_wait(far.at[1], 1)
            for c in y_edges:
                c.start()

    def wait_wind(k, j):
        if j == 3:
            relay[k].wait_recv()
        else:
            direct[j - 1][k].wait_recv()

    def sweep_x(step, j):
        field = (field0, field1)[step]
        turned = (turned0, turned1)[step]
        for n in range(pairs):
            p = member_of(j) * pairs + n
            for h in range(2):
                level = 2 * p + h
                for g in range(width_x // GROUP):
                    taps = [vx[k, level, pl.ds(GROUP * g, GROUP), :] for k in range(TAPS)]
                    for t in range(trac):
                        cells = [
                            field[t, level, pl.ds(GROUP + GROUP * g + s, GROUP), :] for s in range(-RIM, RIM + 1)
                        ]
                        swept[pairs * j + n, t, pl.ds(width_x * h + GROUP * g, GROUP), :] = weighted(taps, cells)
            for t in range(trac):
                turned[t, p, pl.ds(GROUP, width_y), :] = swept[pairs * j + n, t].T

    def sweep_y(step, j, groups):
        turned = (turned0, turned1)[step]
        for n in range(pairs):
            p = member_of(j) * pairs + n
            for g in groups:
                taps = [vy[k, p, pl.ds(GROUP * g, GROUP), :] for k in range(TAPS)]
                for t in range(trac):
                    cells = [turned[t, p, pl.ds(GROUP + GROUP * g + s, GROUP), :] for s in range(-RIM, RIM + 1)]
                    swept[pairs * j + n, t, pl.ds(GROUP * g, GROUP), :] = weighted(taps, cells)

    def turn_back(step, j):
        for n in range(pairs):
            p = member_of(j) * pairs + n
            for t in range(trac):
                done = swept.at[pairs * j + n, t]
                if step == 0:
                    rim_before[t, p] = jnp.where(
                        upper_rows, done[pl.ds(0, GROUP), :], done[pl.ds(width_y - GROUP, GROUP), :]
                    )
                (mid, field_out)[step][t, pl.ds(2 * p, 2)] = done[...].T.reshape(2, width_x, width_y)

    def sweep_z(row):
        def put(t, l, new):
            field1[t, l, pl.ds(GROUP + row, GROUP), :] = new

        column_sweep(mid, fz, row, put)

    def exchange(k):
        direct[1][k].wait_recv()
        relay[k].start()

    wait_wind(0, 1)
    x_taps(1, True)
    load.wait()
    for j in range(4):
        if j == 2:
            exchange(0)
        if j == 3:
            wait_wind(0, 3)
        if j > 1:
            x_taps(j, True)
        x_edges[j].wait_recv()
        x_taps(j, False)
        for c in halos[0][j]:
            c.wait_recv()
        sweep_x(0, j)
        if j == 0:
            ends_are_in()
            for k in range(2, len(parts)):
                direct[1][k].start()
                direct[0][k].start()
        for c in packs[0][j]:
            c.start()
        if j == 0:
            wait_wind(1, 1)
            turn_wind(1)
            y_taps(1, True)
    turn_flux_rims()
    for c in flux_sends:
        c.start()
    for j in range(4):
        if j == 1:
            exchange(1)
            turn_wind(2)
            y_taps(2, True)
        if j == 2:
            wait_wind(1, 3)
            turn_wind(3)
            y_taps(3, True)
            exchange(2)
            exchange(3)
            locals_[2].wait()
            turn_wind_rims(0)
            for k in (2, 3, 4):
                wait_wind(k, 1)
            turn_wind_rims(1)
        y_edges[j].wait_recv()
        y_taps(j, False)
        for c in packs[0][j]:
            c.wait_recv()
        sweep_y(0, j, y_groups)
        turn_back(0, j)
    for k in (2, 3):
        wait_wind(k, 3)
    sweep_z(0)
    sweep_z(width_x - GROUP)
    for j in range(4):
        for c in halos[1][j]:
            c.start()
    exchange(4)
    turn_wind_rims(2)
    wait_wind(4, 3)
    turn_wind_rims(3)
    rim_sweep_z()
    for c in rim_sends:
        c.start()
    winds_on = pltpu.make_async_copy(fz, winds_out, out_sem)
    winds_on.start()

    def one_group(g, carry):
        sweep_z(pl.multiple_of(g * GROUP, GROUP))
        return carry

    lax.fori_loop(1, width_x // GROUP - 1, one_group, 0)

    for c in flux_sends:
        c.wait_recv()
    rim_taps()
    for j in range(4):
        for c in halos[1][j]:
            c.wait_recv()
        sweep_x(1, j)
        sweep_y(1, j, y_groups[1:-1])
    for c in rim_sends:
        c.wait_recv()
    rim_sweep_x()
    for j in range(4):
        sweep_y(1, j, (y_groups[0], y_groups[-1]))
        turn_back(1, j)
    winds_on.wait()

    for step in range(2):
        for j in range(4):
            for c in halos[step][j] + packs[step][j]:
                c.wait_send()
    for c in direct[0] + direct[1] + relay + x_edges + y_edges + flux_sends + rim_sends:
        c.wait_send()


def body(sizes, tracers, flux_x, flux_y, flux_z):
    trac, levels, width_x, width_y = tracers.shape
    members = sizes[0]
    padded = pltpu.VMEM((trac, levels, width_x + 2 * GROUP, width_y), jnp.float32)
    turned = pltpu.VMEM((trac, levels // 2, width_y + 2 * GROUP, 2 * width_x), jnp.float32)
    rims = pltpu.VMEM((trac, levels // 2, GROUP, LANES), jnp.float32)
    flux_rims = pltpu.VMEM((2, levels // 2, GROUP, LANES), jnp.float32)
    block = pltpu.VMEM((levels, width_x, width_y), jnp.float32)
    swept, winds = pl.pallas_call(
        functools.partial(kernel, sizes),
        out_shape=[
            pltpu.VMEM(tracers.shape, jnp.float32),
            pltpu.VMEM((levels, width_x, width_y), jnp.float32),
        ],
        in_specs=[pl.BlockSpec(memory_space=pltpu.HBM)] * 4,
        out_specs=[pl.BlockSpec(memory_space=pltpu.VMEM)] * 2,
        scratch_shapes=[
            padded,
            padded,
            turned,
            turned,
            pltpu.VMEM((trac, levels, width_x, width_y), jnp.float32),
            pltpu.VMEM((levels, width_x + GROUP, width_y), jnp.float32),
            block,
            block,
            pltpu.VMEM((levels // 2, width_y + GROUP, 2 * width_x), jnp.float32),
            pltpu.VMEM((TAPS, levels, width_x, width_y), jnp.float32),
            pltpu.VMEM((TAPS, levels // 2, width_y, 2 * width_x), jnp.float32),
            pltpu.VMEM((FACE, width_y + GROUP, LANES), jnp.float32),
            pltpu.VMEM((levels // 2, trac, 2 * width_x, width_y), jnp.float32),
            rims,
            rims,
            flux_rims,
            flux_rims,
            rims,
            pltpu.VMEM((trac, GROUP, LANES), jnp.float32),
            pltpu.VMEM((2, trac, GROUP, LANES), jnp.float32),
            pltpu.VMEM((TAPS, levels // 2, GROUP, LANES), jnp.float32),
            pltpu.VMEM((levels // 2, GROUP, LANES), jnp.float32),
            pltpu.SemaphoreType.DMA((4,)),
            pltpu.SemaphoreType.DMA((3, 5)),
            pltpu.SemaphoreType.DMA((3, 5)),
            pltpu.SemaphoreType.DMA((2, 4)),
            pltpu.SemaphoreType.DMA((2, 4)),
            pltpu.SemaphoreType.DMA((2, 4, 2)),
            pltpu.SemaphoreType.DMA((2, 4, 2)),
            pltpu.SemaphoreType.DMA((2, 4, 2)),
            pltpu.SemaphoreType.DMA((2, 4, 2)),
            pltpu.SemaphoreType.DMA,
            pltpu.SemaphoreType.REGULAR((2,)),
            pltpu.SemaphoreType.REGULAR((2,)),
            pltpu.SemaphoreType.DMA((8,)),
            pltpu.SemaphoreType.DMA((8,)),
        ],
        compiler_params=pltpu.CompilerParams(
            collective_id=0, has_side_effects=True, vmem_limit_bytes=40 * 2**20
        ),
    )(*(pltpu.with_memory_space_constraint(a, pltpu.HBM) for a in (tracers, flux_x, flux_y, flux_z)))
    return pl.pallas_call(
        last_kernel,
        out_shape=jax.ShapeDtypeStruct(tracers.shape, jnp.float32),
        in_specs=[pl.BlockSpec(memory_space=pltpu.VMEM)] * 2,
        out_specs=pl.BlockSpec(memory_space=pl.ANY),
        scratch_shapes=[
            pltpu.VMEM(tracers.shape, jnp.float32),
            pltpu.SemaphoreType.DMA((width_x // GROUP,)),
        ],
        compiler_params=pltpu.CompilerParams(vmem_limit_bytes=8 * 2**20),
    )(swept, winds)


def solution(mesh):
    sizes = (mesh.shape["member"], mesh.shape["gx"], mesh.shape["gy"])
    return jax.shard_map(
        functools.partial(body, sizes),
        mesh=mesh,
        in_specs=(
            P("member", None, "gx", "gy"),
            P("member", "gx", "gy"),
            P("member", "gx", "gy"),
            P("member", "gx", "gy"),
        ),
        out_specs=P("member", None, "gx", "gy"),
        check_vma=False,
    )
```

```python
import functools

import jax
import jax.numpy as jnp
from jax import lax
from jax.experimental import pallas as pl
from jax.experimental.pallas import tpu as pltpu
from jax.sharding import PartitionSpec as P

MESH = pl.DeviceIdType.MESH
LANES = 128
GROUP = 8
RIM = 3
TAPS = 2 * RIM + 1
FACE = 2 * RIM


def coefficients(c):
    s = jnp.abs(c)
    t = 1.0 - s
    ct = c * t * (1.0 / 12.0)
    return c > 0, ct * t, ct * s, c * s * (3.0 - 2.0 * s)


def flux(coefs, e, o, upwind):
    _, near, far, mean = coefs
    return near * e - far * o + mean * upwind


def face_weights(c):
    positive, near, far, mean = coefficients(c)
    near7 = 7.0 * near
    far7 = 7.0 * far
    second = -(near + far7)
    upwind = near7 - far7 + mean
    downwind = near7 + far
    last = -near
    zero = jnp.zeros_like(c)
    return (
        jnp.where(positive, far, zero),
        jnp.where(positive, second, last),
        jnp.where(positive, upwind, downwind),
        jnp.where(positive, downwind, upwind),
        jnp.where(positive, last, second),
        jnp.where(positive, zero, far),
    )


def cell_taps(low, high):
    taps = [low[0]]
    for k in range(1, FACE):
        taps.append(low[k] - high[k - 1])
    taps.append(-high[FACE - 1])
    taps[RIM] = taps[RIM] + 1.0
    return taps


def weighted(taps, cells):
    terms = [a * b for a, b in zip(taps, cells)]
    while len(terms) > 1:
        terms = [sum(terms[i : i + 2]) if i + 1 < len(terms) else terms[i] for i in range(0, len(terms), 2)]
    return terms[0]


def column_sweep(field, winds, row, put):
    trac, levels = field.shape[0], field.shape[1]
    q = {}
    p = {}
    e = {}
    before = {}

    def cell(t, l):
        l = min(max(l, 0), levels - 1)
        if (t, l) not in q:
            q[t, l] = field[t, l, pl.ds(row, GROUP), :]
        return q[t, l]

    def pair(t, l):
        if (t, l) not in p:
            p[t, l] = cell(t, l - 1) + cell(t, l)
        return p[t, l]

    def edge(t, l):
        if (t, l) not in e:
            e[t, l] = 8.0 * pair(t, l) - (pair(t, l - 1) + pair(t, l + 1))
        return e[t, l]

    for l in range(levels):
        if l + 1 < levels:
            coefs = coefficients(winds[l, pl.ds(row, GROUP), :])
        for t in range(trac):
            new = cell(t, l)
            if l > 0:
                new = new + before[t]
            if l + 1 < levels:
                positive = coefs[0]
                o = jnp.where(positive, edge(t, l), edge(t, l + 2))
                f = flux(coefs, edge(t, l + 1), o, jnp.where(positive, cell(t, l), cell(t, l + 1)))
                new = new - f
                before[t] = f
            put(t, l, new)


def last_kernel(field, winds, out, staged, out_sem):
    def store(row):
        rows = pl.ds(row, GROUP)
        return pltpu.make_async_copy(staged.at[:, :, rows, :], out.at[:, :, rows, :], out_sem.at[row // GROUP])

    def one_group(g, carry):
        row = pl.multiple_of(g * GROUP, GROUP)

        def put(t, l, new):
            staged[t, l, pl.ds(row, GROUP), :] = new

        column_sweep(field, winds, row, put)
        store(row).start()
        return carry

    groups = field.shape[2] // GROUP
    lax.fori_loop(0, groups, one_group, 0)
    for g in range(groups):
        store(g * GROUP).wait()


def kernel(
    sizes,
    tracers,
    flux_x,
    flux_y,
    flux_z,
    field_out,
    winds_out,
    field0,
    field1,
    turned0,
    turned1,
    mid,
    fx,
    fy,
    fz,
    fyt,
    vx,
    vy,
    face,
    swept,
    rim_before,
    rim_after,
    rim_flux,
    far_flux,
    far_rim,
    corner,
    far_corner,
    far_taps,
    rim_winds,
    local_sem,
    wind_send,
    wind_recv,
    edge_send,
    edge_recv,
    halo_send,
    halo_recv,
    pack_send,
    pack_recv,
    out_sem,
    far,
    known,
    rim_send,
    rim_recv,
):
    members, n_x, n_y = sizes
    trac, levels, width_x, width_y = tracers.shape
    slab = levels // members
    pairs = slab // 2
    m = lax.axis_index("member")
    ix = lax.axis_index("gx")
    iy = lax.axis_index("gy")

    def member_of(j):
        if j == 0:
            return m
        if j == 1:
            return m + 1 - 2 * lax.rem(m, 2)
        if j == 2:
            return lax.rem(m + 2, 4)
        return 3 - m

    def device(j, dx, dy):
        return (member_of(j), lax.rem(ix + dx + n_x, n_x), lax.rem(iy + dy + n_y, n_y))

    last = n_y - 1
    barrier = pltpu.get_barrier_semaphore()
    x_steps = (1,) if n_x == 2 else (1, -1)
    near = [(1, 0, 0), (2, 0, 0), (3, 0, 0)] + [(0, d, 0) for d in x_steps]
    up = (0, 0, 1)
    down = (0, 0, -1)

    def signal(semaphore, partner):
        pl.semaphore_signal(semaphore, inc=1, device_id=device(*partner), device_id_type=MESH)

    for partner in near:
        signal(barrier, partner)
    pl.when(iy < last)(lambda: signal(barrier, up))
    pl.when(iy > 0)(lambda: signal(barrier, down))

    def levels_of(j):
        return pl.ds(member_of(j) * slab, slab)

    def pairs_of(j):
        return pl.ds(member_of(j) * pairs, pairs)

    inner = pl.ds(GROUP, width_x)
    every = (0, width_x)
    parts = (
        (flux_x, fx, GROUP, every),
        (flux_y, fy, 0, every),
        (flux_z, fz, 0, (0, GROUP)),
        (flux_z, fz, 0, (width_x - GROUP, GROUP)),
        (flux_z, fz, 0, (GROUP, width_x - 2 * GROUP)),
    )

    def wind_src(k):
        start, size = parts[k][3]
        return parts[k][0].at[:, pl.ds(start, size), :]

    def wind_dst(k, j):
        _, block, offset, (start, size) = parts[k]
        return block.at[levels_of(j), pl.ds(offset + start, size), :]

    locals_ = [
        pltpu.make_async_copy(flux_x, fx.at[levels_of(0), inner, :], local_sem.at[0]),
        pltpu.make_async_copy(flux_y, fy.at[levels_of(0)], local_sem.at[1]),
        pltpu.make_async_copy(flux_z, fz.at[levels_of(0)], local_sem.at[2]),
    ]
    load = pltpu.make_async_copy(tracers, field0.at[:, :, inner, :], local_sem.at[3])
    locals_[1].start()
    locals_[0].start()
    load.start()
    locals_[2].start()

    def remote(src, dst, send, recv, dev):
        return pltpu.make_async_remote_copy(
            src_ref=src, dst_ref=dst, send_sem=send, recv_sem=recv, device_id=dev, device_id_type=MESH
        )

    def halo_copies(step, j):
        target = (field0, field1)[step]
        ls = levels_of(j)
        if step == 0:
            low_src = tracers.at[:, ls, pl.ds(0, RIM), :]
            high_src = tracers.at[:, ls, pl.ds(width_x - RIM, RIM), :]
        else:
            low_src = field1.at[:, ls, pl.ds(GROUP, RIM), :]
            high_src = field1.at[:, ls, pl.ds(GROUP + width_x - RIM, RIM), :]
        return (
            remote(
                high_src,
                target.at[:, ls, pl.ds(GROUP - RIM, RIM), :],
                halo_send.at[step, j, 0],
                halo_recv.at[step, j, 0],
                device(0, 1, 0),
            ),
            remote(
                low_src,
                target.at[:, ls, pl.ds(width_x + GROUP, RIM), :],
                halo_send.at[step, j, 1],
                halo_recv.at[step, j, 1],
                device(0, -1, 0),
            ),
        )

    def pack_copies(step, j):
        turned = (turned0, turned1)[step]
        ps = pairs_of(j)
        return (
            remote(
                turned.at[:, ps, pl.ds(GROUP + width_y - RIM, RIM), :],
                turned.at[:, ps, pl.ds(GROUP - RIM, RIM), :],
                pack_send.at[step, j, 0],
                pack_recv.at[step, j, 0],
                device(0, 0, 1),
            ),
            remote(
                turned.at[:, ps, pl.ds(GROUP, RIM), :],
                turned.at[:, ps, pl.ds(GROUP + width_y, RIM), :],
                pack_send.at[step, j, 1],
                pack_recv.at[step, j, 1],
                device(0, 0, -1),
            ),
        )

    halos = [[halo_copies(step, j) for j in range(4)] for step in range(2)]
    packs = [[pack_copies(0, j) for j in range(4)], [() for j in range(4)]]
    above = pl.ds(0, RIM)
    below = pl.ds(GROUP - RIM, RIM)

    def rim_pair(src, dst, n, dx):
        return [
            remote(
                src.at[..., rows, :], dst.at[..., rows, :], rim_send.at[n + i], rim_recv.at[n + i], device(0, dx, dy)
            )
            for i, (rows, dy) in enumerate(((below, 1), (above, -1)))
        ]

    flux_sends = rim_pair(rim_flux, far_flux, 0, 0)
    rim_sends = []
    for t in range(trac):
        first = 2 + 6 * t
        sends = rim_pair(rim_after.at[t], far_rim.at[t], first, 0)
        sends += rim_pair(corner.at[t], far_corner.at[0, t], first + 2, 1)
        if n_x > 2:
            sends += rim_pair(corner.at[t], far_corner.at[1, t], first + 4, -1)
        rim_sends.append(sends)

    lane = lax.broadcasted_iota(jnp.int32, (GROUP, LANES), 1)
    first_half = lane < width_x
    across = lax.rem(lane, width_x)
    slot = lax.rem(lane + LANES - (width_x - RIM), width_x)
    upper_rows = lax.broadcasted_iota(jnp.int32, (GROUP, LANES), 0) < GROUP // 2
    n_pairs = levels // 2
    y_groups = tuple(range(width_y // GROUP))

    def rim_of(tile):
        return jnp.where(upper_rows, tile[:GROUP], tile[width_y - GROUP :])

    def turn_flux_rims():
        def one_pair(p, carry):
            for u in range(2):
                both = fx[pl.ds(2 * p, 2), pl.ds(GROUP - 1 + u, width_x), :]
                rim_flux[u, p] = rim_of(both.reshape(2 * width_x, width_y).T)
            return carry

        lax.fori_loop(0, n_pairs, one_pair, 0)

    def rim_taps():
        for p in range(n_pairs):
            taps = cell_taps(face_weights(far_flux[0, p]), face_weights(far_flux[1, p]))
            for k in range(TAPS):
                far_taps[k, p] = taps[k]

    def turn_wind_rims(j):
        for n in range(pairs):
            p = member_of(j) * pairs + n
            rim_winds[p] = rim_of(fz[pl.ds(2 * p, 2)].reshape(2 * width_x, width_y).T)

    def rim_sweep_z():
        winds_at = [rim_winds[p] for p in range(n_pairs)]
        winds_at[-1] = jnp.where(first_half, winds_at[-1], 0.0)

        def swap(x):
            return pltpu.roll(x, width_x, 1)

        for t in range(trac):
            q = [rim_before[t, p] for p in range(n_pairs)]
            r = [swap(x) for x in q]
            top = jnp.where(first_half, q[0], r[0])
            bottom = jnp.where(first_half, r[-1], q[-1])

            def at(rows, p):
                return top if p < 0 else bottom if p >= n_pairs else rows[p]

            def next_level(p):
                return jnp.where(first_half, at(r, p), at(r, p + 1))

            flows = []
            for p in range(n_pairs):
                cells = [
                    at(q, p - 1),
                    jnp.where(first_half, at(r, p - 1), r[p]),
                    q[p],
                    next_level(p),
                    at(q, p + 1),
                    next_level(p + 1),
                ]
                flows.append(weighted(face_weights(winds_at[p]), cells))
            turned_flows = [swap(f) for f in flows]
            packed = None
            for p in range(n_pairs):
                earlier = turned_flows[p - 1] if p else jnp.zeros_like(top)
                new = q[p] + (jnp.where(first_half, earlier, turned_flows[p]) - flows[p])
                rim_after[t, p] = new
                moved = pltpu.roll(new, GROUP * p, 1) if p else new
                packed = moved if packed is None else jnp.where(slot // GROUP == p, moved, packed)
            corner[t] = packed
            for c in rim_sends[t]:
                c.start()

    def rim_sweep_x():
        for t in range(trac):
            for c in rim_sends[t]:
                c.wait_recv()
            beyond = far_corner[0, t]
            if n_x > 2:
                beyond = jnp.where(lax.rem(slot, GROUP) < RIM, beyond, far_corner[1, t])
            for p in range(n_pairs):
                own = far_rim[t, p]
                other = pltpu.roll(beyond, (width_x - GROUP * p) % LANES, 1)
                cells = []
                for d in range(-RIM, RIM + 1):
                    if d == 0:
                        cells.append(own)
                        continue
                    inside = (across + d >= 0) & (across + d < width_x)
                    cells.append(
                        jnp.where(inside, pltpu.roll(own, -d % LANES, 1), pltpu.roll(other, -d % LANES, 1))
                    )
                new = weighted([far_taps[k, p] for k in range(TAPS)], cells)
                turned1[t, p, pl.ds(GROUP - RIM, RIM), :] = new[GROUP - RIM :]
                turned1[t, p, pl.ds(GROUP + width_y, RIM), :] = new[:RIM]

    direct = [
        [
            remote(wind_src(k), wind_dst(k, 0), wind_send.at[j - 1, k], wind_recv.at[j - 1, k], device(j, 0, 0))
            for k in range(len(parts))
        ]
        for j in (1, 2)
    ]
    relay = [
        remote(wind_dst(k, 2), wind_dst(k, 2), wind_send.at[2, k], wind_recv.at[2, k], device(1, 0, 0))
        for k in range(len(parts))
    ]

    x_edges = [
        remote(
            flux_x.at[:, pl.ds(width_x - 1, 1), :],
            fx.at[levels_of(0), pl.ds(GROUP - 1, 1), :],
            edge_send.at[0, j],
            edge_recv.at[0, j],
            device(j, 1, 0),
        )
        for j in range(4)
    ]
    y_edges = [
        remote(
            fyt.at[pairs_of(0), pl.ds(GROUP + width_y - 1, 1), :],
            fyt.at[pairs_of(0), pl.ds(GROUP - 1, 1), :],
            edge_send.at[1, j],
            edge_recv.at[1, j],
            device(j, 0, 1),
        )
        for j in range(4)
    ]

    def turn_wind(j):
        first = member_of(j) * pairs

        def one_pair(k, carry):
            p = first + k
            both = fy[pl.ds(2 * p, 2)].reshape(2 * width_x, width_y)
            fyt[p, pl.ds(GROUP, width_y), :] = both.T
            return carry

        lax.fori_loop(0, pairs, one_pair, 0)

    def put_faces(read, start, row):
        for k, w in enumerate(face_weights(read(start))):
            face[k, pl.ds(row, GROUP), :] = w

    def put_taps(store, g, row):
        low = [face[k, pl.ds(row, GROUP), :] for k in range(FACE)]
        high = [face[k, pl.ds(row + 1, GROUP), :] for k in range(FACE)]
        for k, tap in enumerate(cell_taps(low, high)):
            store(k, g, tap)

    def inner_taps(read, store, extent):
        for g in range(extent // GROUP):
            put_faces(read, GROUP * g + 1, GROUP * g + GROUP)
        for g in range(1, extent // GROUP):
            put_taps(store, g, GROUP * g + GROUP - 1)

    def first_taps(read, store):
        put_faces(read, 0, 0)
        put_faces(read, 1, 1)
        put_taps(store, 0, 0)

    def x_taps(j, inside):
        first = member_of(j) * slab

        def one_level(n, carry):
            level = first + n

            def read(start):
                return fx[level, pl.ds(GROUP - 1 + start, GROUP), :]

            def store(k, g, tap):
                vx[k, level, pl.ds(GROUP * g, GROUP), :] = tap

            if inside:
                inner_taps(read, store, width_x)
            else:
                first_taps(read, store)
            return carry

        lax.fori_loop(0, slab, one_level, 0)

    def y_taps(j, inside):
        first = member_of(j) * pairs

        def one_pair(n, carry):
            p = first + n

            def read(start):
                return fyt[p, pl.ds(GROUP - 1 + start, GROUP), :]

            def store(k, g, tap):
                vy[k, p, pl.ds(GROUP * g, GROUP), :] = tap

            if inside:
                inner_taps(read, store, width_y)
            else:
                first_taps(read, store)
            return carry

        lax.fori_loop(0, pairs, one_pair, 0)

    locals_[1].wait()
    turn_wind(0)
    pl.semaphore_wait(barrier, len(near) + lax.min(iy, 1) + lax.min(last - iy, 1))
    signal(known.at[0], (0, -1, 0))
    pl.when(iy > 0)(lambda: signal(known.at[1], down))
    pl.when(iy == 0)(lambda: signal(far.at[1], up))
    pl.when(iy == last - 1)(lambda: signal(far.at[0], down))
    direct[1][0].start()
    x_edges[0].start()
    for c in halos[0][0]:
        c.start()
    direct[0][0].start()
    for j in range(1, 4):
        for c in halos[0][j]:
            c.start()

    locals_[0].wait()
    x_taps(0, True)
    y_taps(0, True)

    pl.semaphore_wait(known.at[0], 1)
    for c in x_edges[1:]:
        c.start()

    @pl.when(iy < last)
    def _():
        pl.semaphore_wait(known.at[1], 1)
        for c in y_edges:
            c.start()

    for k in range(1, len(parts)):
        direct[1][k].start()
        direct[0][k].start()

    @pl.when((iy > 0) & (iy < last - 1))
    def _():
        pl.semaphore_wait(far.at[0], 1)
        signal(far.at[0], down)

    @pl.when((iy > 0) & (iy < last))
    def _():
        pl.semaphore_wait(far.at[1], 1)
        signal(far.at[1], up)

    def ends_are_in():
        @pl.when(iy == 0)
        def _():
            pl.semaphore_wait(far.at[0], 1)

        @pl.when(iy == last)
        def _():
            pl.semaphore_wait(far.at[1], 1)
            for c in y_edges:
                c.start()

    def wait_wind(k, j):
        if j == 3:
            relay[k].wait_recv()
        else:
            direct[j - 1][k].wait_recv()

    def sweep_x(step, j):
        field = (field0, field1)[step]
        turned = (turned0, turned1)[step]
        for n in range(pairs):
            p = member_of(j) * pairs + n
            for h in range(2):
                level = 2 * p + h
                for g in range(width_x // GROUP):
                    taps = [vx[k, level, pl.ds(GROUP * g, GROUP), :] for k in range(TAPS)]
                    for t in range(trac):
                        cells = [
                            field[t, level, pl.ds(GROUP + GROUP * g + s, GROUP), :] for s in range(-RIM, RIM + 1)
                        ]
                        swept[pairs * j + n, t, pl.ds(width_x * h + GROUP * g, GROUP), :] = weighted(taps, cells)
            for t in range(trac):
                turned[t, p, pl.ds(GROUP, width_y), :] = swept[pairs * j + n, t].T

    def sweep_y(step, j, groups):
        turned = (turned0, turned1)[step]
        for n in range(pairs):
            p = member_of(j) * pairs + n
            for g in groups:
                taps = [vy[k, p, pl.ds(GROUP * g, GROUP), :] for k in range(TAPS)]
                for t in range(trac):
                    cells = [turned[t, p, pl.ds(GROUP + GROUP * g + s, GROUP), :] for s in range(-RIM, RIM + 1)]
                    swept[pairs * j + n, t, pl.ds(GROUP * g, GROUP), :] = weighted(taps, cells)

    def turn_back(step, j):
        for n in range(pairs):
            p = member_of(j) * pairs + n
            for t in range(trac):
                done = swept.at[pairs * j + n, t]
                if step == 0:
                    rim_before[t, p] = jnp.where(
                        upper_rows, done[pl.ds(0, GROUP), :], done[pl.ds(width_y - GROUP, GROUP), :]
                    )
                (mid, field_out)[step][t, pl.ds(2 * p, 2)] = done[...].T.reshape(2, width_x, width_y)

    def sweep_z(row):
        def put(t, l, new):
            field1[t, l, pl.ds(GROUP + row, GROUP), :] = new

        column_sweep(mid, fz, row, put)

    def exchange(k):
        direct[1][k].wait_recv()
        relay[k].start()

    wait_wind(0, 1)
    x_taps(1, True)
    load.wait()
    for j in range(4):
        if j == 2:
            exchange(0)
        if j == 3:
            wait_wind(0, 3)
        if j > 1:
            x_taps(j, True)
        x_edges[j].wait_recv()
        x_taps(j, False)
        for c in halos[0][j]:
            c.wait_recv()
        sweep_x(0, j)
        if j == 0:
            ends_are_in()
        for c in packs[0][j]:
            c.start()
        if j == 0:
            wait_wind(1, 1)
            turn_wind(1)
            y_taps(1, True)
    turn_flux_rims()
    for c in flux_sends:
        c.start()
    for j in range(4):
        if j == 1:
            exchange(1)
            turn_wind(2)
            y_taps(2, True)
        if j == 2:
            wait_wind(1, 3)
            turn_wind(3)
            y_taps(3, True)
            exchange(2)
            exchange(3)
            locals_[2].wait()
            turn_wind_rims(0)
            for k in (2, 3, 4):
                wait_wind(k, 1)
            turn_wind_rims(1)
        sweep_y(0, j, y_groups[1:-1])
    for j in range(4):
        y_edges[j].wait_recv()
        y_taps(j, False)
        for c in packs[0][j]:
            c.wait_recv()
        sweep_y(0, j, (y_groups[0], y_groups[-1]))
        turn_back(0, j)
    for k in (2, 3):
        wait_wind(k, 3)
    sweep_z(0)
    sweep_z(width_x - GROUP)
    for j in range(4):
        for c in halos[1][j]:
            c.start()
    exchange(4)
    turn_wind_rims(2)
    wait_wind(4, 3)
    turn_wind_rims(3)
    rim_sweep_z()
    winds_on = pltpu.make_async_copy(fz, winds_out, out_sem)
    winds_on.start()

    def one_group(g, carry):
        sweep_z(pl.multiple_of(g * GROUP, GROUP))
        return carry

    lax.fori_loop(1, width_x // GROUP - 1, one_group, 0)

    for c in flux_sends:
        c.wait_recv()
    rim_taps()
    for j in range(4):
        for c in halos[1][j]:
            c.wait_recv()
        sweep_x(1, j)
        sweep_y(1, j, y_groups[1:-1])
    rim_sweep_x()
    for j in range(4):
        sweep_y(1, j, (y_groups[0], y_groups[-1]))
        turn_back(1, j)
    winds_on.wait()

    for step in range(2):
        for j in range(4):
            for c in halos[step][j] + packs[step][j]:
                c.wait_send()
    for c in direct[0] + direct[1] + relay + x_edges + y_edges + flux_sends + sum(rim_sends, []):
        c.wait_send()


def body(sizes, tracers, flux_x, flux_y, flux_z):
    trac, levels, width_x, width_y = tracers.shape
    members = sizes[0]
    padded = pltpu.VMEM((trac, levels, width_x + 2 * GROUP, width_y), jnp.float32)
    turned = pltpu.VMEM((trac, levels // 2, width_y + 2 * GROUP, 2 * width_x), jnp.float32)
    rims = pltpu.VMEM((trac, levels // 2, GROUP, LANES), jnp.float32)
    flux_rims = pltpu.VMEM((2, levels // 2, GROUP, LANES), jnp.float32)
    block = pltpu.VMEM((levels, width_x, width_y), jnp.float32)
    swept, winds = pl.pallas_call(
        functools.partial(kernel, sizes),
        out_shape=[
            pltpu.VMEM(tracers.shape, jnp.float32),
            pltpu.VMEM((levels, width_x, width_y), jnp.float32),
        ],
        in_specs=[pl.BlockSpec(memory_space=pltpu.HBM)] * 4,
        out_specs=[pl.BlockSpec(memory_space=pltpu.VMEM)] * 2,
        scratch_shapes=[
            padded,
            padded,
            turned,
            turned,
            pltpu.VMEM((trac, levels, width_x, width_y), jnp.float32),
            pltpu.VMEM((levels, width_x + GROUP, width_y), jnp.float32),
            block,
            block,
            pltpu.VMEM((levels // 2, width_y + GROUP, 2 * width_x), jnp.float32),
            pltpu.VMEM((TAPS, levels, width_x, width_y), jnp.float32),
            pltpu.VMEM((TAPS, levels // 2, width_y, 2 * width_x), jnp.float32),
            pltpu.VMEM((FACE, width_y + GROUP, LANES), jnp.float32),
            pltpu.VMEM((levels // 2, trac, 2 * width_x, width_y), jnp.float32),
            rims,
            rims,
            flux_rims,
            flux_rims,
            rims,
            pltpu.VMEM((trac, GROUP, LANES), jnp.float32),
            pltpu.VMEM((2, trac, GROUP, LANES), jnp.float32),
            pltpu.VMEM((TAPS, levels // 2, GROUP, LANES), jnp.float32),
            pltpu.VMEM((levels // 2, GROUP, LANES), jnp.float32),
            pltpu.SemaphoreType.DMA((4,)),
            pltpu.SemaphoreType.DMA((3, 5)),
            pltpu.SemaphoreType.DMA((3, 5)),
            pltpu.SemaphoreType.DMA((2, 4)),
            pltpu.SemaphoreType.DMA((2, 4)),
            pltpu.SemaphoreType.DMA((2, 4, 2)),
            pltpu.SemaphoreType.DMA((2, 4, 2)),
            pltpu.SemaphoreType.DMA((2, 4, 2)),
            pltpu.SemaphoreType.DMA((2, 4, 2)),
            pltpu.SemaphoreType.DMA,
            pltpu.SemaphoreType.REGULAR((2,)),
            pltpu.SemaphoreType.REGULAR((2,)),
            pltpu.SemaphoreType.DMA((14,)),
            pltpu.SemaphoreType.DMA((14,)),
        ],
        compiler_params=pltpu.CompilerParams(
            collective_id=0, has_side_effects=True, vmem_limit_bytes=40 * 2**20
        ),
    )(*(pltpu.with_memory_space_constraint(a, pltpu.HBM) for a in (tracers, flux_x, flux_y, flux_z)))
    return pl.pallas_call(
        last_kernel,
        out_shape=jax.ShapeDtypeStruct(tracers.shape, jnp.float32),
        in_specs=[pl.BlockSpec(memory_space=pltpu.VMEM)] * 2,
        out_specs=pl.BlockSpec(memory_space=pl.ANY),
        scratch_shapes=[
            pltpu.VMEM(tracers.shape, jnp.float32),
            pltpu.SemaphoreType.DMA((width_x // GROUP,)),
        ],
        compiler_params=pltpu.CompilerParams(vmem_limit_bytes=8 * 2**20),
    )(swept, winds)


def solution(mesh):
    sizes = (mesh.shape["member"], mesh.shape["gx"], mesh.shape["gy"])
    return jax.shard_map(
        functools.partial(body, sizes),
        mesh=mesh,
        in_specs=(
            P("member", None, "gx", "gy"),
            P("member", "gx", "gy"),
            P("member", "gx", "gy"),
            P("member", "gx", "gy"),
        ),
        out_specs=P("member", None, "gx", "gy"),
        check_vma=False,
    )
```

```python
import functools

import jax
import jax.numpy as jnp
from jax import lax
from jax.experimental import pallas as pl
from jax.experimental.pallas import tpu as pltpu
from jax.sharding import PartitionSpec as P

MESH = pl.DeviceIdType.MESH
LANES = 128
GROUP = 8
RIM = 3
TAPS = 2 * RIM + 1
FACE = 2 * RIM
TAIL = 12


def coefficients(c):
    s = jnp.abs(c)
    t = 1.0 - s
    ct = c * t * (1.0 / 12.0)
    return c > 0, ct * t, ct * s, c * s * (3.0 - 2.0 * s)


def flux(coefs, e, o, upwind):
    _, near, far, mean = coefs
    return near * e - far * o + mean * upwind


def face_weights(c):
    positive, near, far, mean = coefficients(c)
    near7 = 7.0 * near
    far7 = 7.0 * far
    second = -(near + far7)
    upwind = near7 - far7 + mean
    downwind = near7 + far
    last = -near
    zero = jnp.zeros_like(c)
    return (
        jnp.where(positive, far, zero),
        jnp.where(positive, second, last),
        jnp.where(positive, upwind, downwind),
        jnp.where(positive, downwind, upwind),
        jnp.where(positive, last, second),
        jnp.where(positive, zero, far),
    )


def cell_taps(low, high):
    taps = [low[0]]
    for k in range(1, FACE):
        taps.append(low[k] - high[k - 1])
    taps.append(-high[FACE - 1])
    taps[RIM] = taps[RIM] + 1.0
    return taps


def weighted(taps, cells):
    terms = [a * b for a, b in zip(taps, cells)]
    while len(terms) > 1:
        terms = [sum(terms[i : i + 2]) if i + 1 < len(terms) else terms[i] for i in range(0, len(terms), 2)]
    return terms[0]


def column_sweep(field, winds, row, put):
    trac, levels = field.shape[0], field.shape[1]
    q = {}
    p = {}
    e = {}
    before = {}

    def cell(t, l):
        l = min(max(l, 0), levels - 1)
        if (t, l) not in q:
            q[t, l] = field[t, l, pl.ds(row, GROUP), :]
        return q[t, l]

    def pair(t, l):
        if (t, l) not in p:
            p[t, l] = cell(t, l - 1) + cell(t, l)
        return p[t, l]

    def edge(t, l):
        if (t, l) not in e:
            e[t, l] = 8.0 * pair(t, l) - (pair(t, l - 1) + pair(t, l + 1))
        return e[t, l]

    for l in range(levels):
        if l + 1 < levels:
            coefs = coefficients(winds[l, pl.ds(row, GROUP), :])
        for t in range(trac):
            new = cell(t, l)
            if l > 0:
                new = new + before[t]
            if l + 1 < levels:
                positive = coefs[0]
                o = jnp.where(positive, edge(t, l), edge(t, l + 2))
                f = flux(coefs, edge(t, l + 1), o, jnp.where(positive, cell(t, l), cell(t, l + 1)))
                new = new - f
                before[t] = f
            put(t, l, new)


def last_kernel(field, winds, out, staged, out_sem):
    def store(row):
        rows = pl.ds(row, GROUP)
        return pltpu.make_async_copy(staged.at[:, :, rows, :], out.at[:, :, rows, :], out_sem.at[row // GROUP])

    def one_group(g, carry):
        row = pl.multiple_of(g * GROUP, GROUP)

        def put(t, l, new):
            staged[t, l, pl.ds(row, GROUP), :] = new

        column_sweep(field, winds, row, put)
        store(row).start()
        return carry

    groups = field.shape[2] // GROUP
    lax.fori_loop(0, groups, one_group, 0)
    for g in range(groups):
        store(g * GROUP).wait()


def kernel(
    sizes,
    tracers,
    flux_x,
    flux_y,
    flux_z,
    field_out,
    winds_out,
    field0,
    field1,
    turned0,
    turned1,
    mid,
    fx,
    fy,
    fz,
    fyt,
    vx,
    vy,
    face,
    swept,
    rim_before,
    rim_after,
    rim_flux,
    far_flux,
    far_rim,
    corner,
    far_corner,
    far_taps,
    rim_winds,
    local_sem,
    wind_send,
    wind_recv,
    edge_send,
    edge_recv,
    halo_send,
    halo_recv,
    pack_send,
    pack_recv,
    out_sem,
    far,
    known,
    rim_send,
    rim_recv,
):
    members, n_x, n_y = sizes
    trac, levels, width_x, width_y = tracers.shape
    slab = levels // members
    pairs = slab // 2
    m = lax.axis_index("member")
    ix = lax.axis_index("gx")
    iy = lax.axis_index("gy")

    def member_of(j):
        if j == 0:
            return m
        if j == 1:
            return m + 1 - 2 * lax.rem(m, 2)
        if j == 2:
            return lax.rem(m + 2, 4)
        return 3 - m

    def device(j, dx, dy):
        return (member_of(j), lax.rem(ix + dx + n_x, n_x), lax.rem(iy + dy + n_y, n_y))

    last = n_y - 1
    barrier = pltpu.get_barrier_semaphore()
    x_steps = (1,) if n_x == 2 else (1, -1)
    near = [(1, 0, 0), (2, 0, 0), (3, 0, 0)] + [(0, d, 0) for d in x_steps]
    up = (0, 0, 1)
    down = (0, 0, -1)

    def signal(semaphore, partner):
        pl.semaphore_signal(semaphore, inc=1, device_id=device(*partner), device_id_type=MESH)

    for partner in near:
        signal(barrier, partner)
    pl.when(iy < last)(lambda: signal(barrier, up))
    pl.when(iy > 0)(lambda: signal(barrier, down))

    def levels_of(j):
        return pl.ds(member_of(j) * slab, slab)

    def pairs_of(j):
        return pl.ds(member_of(j) * pairs, pairs)

    inner = pl.ds(GROUP, width_x)
    every = (0, width_x)
    parts = (
        (flux_x, fx, GROUP, every),
        (flux_y, fy, 0, every),
        (flux_z, fz, 0, (0, GROUP)),
        (flux_z, fz, 0, (width_x - GROUP, GROUP)),
        (flux_z, fz, 0, (GROUP, width_x - 2 * GROUP - TAIL)),
        (flux_z, fz, 0, (width_x - GROUP - TAIL, TAIL)),
    )

    def wind_src(k):
        start, size = parts[k][3]
        return parts[k][0].at[:, pl.ds(start, size), :]

    def wind_dst(k, j):
        _, block, offset, (start, size) = parts[k]
        return block.at[levels_of(j), pl.ds(offset + start, size), :]

    locals_ = [
        pltpu.make_async_copy(flux_x, fx.at[levels_of(0), inner, :], local_sem.at[0]),
        pltpu.make_async_copy(flux_y, fy.at[levels_of(0)], local_sem.at[1]),
        pltpu.make_async_copy(flux_z, fz.at[levels_of(0)], local_sem.at[2]),
    ]
    load = pltpu.make_async_copy(tracers, field0.at[:, :, inner, :], local_sem.at[3])
    locals_[1].start()
    locals_[0].start()
    load.start()
    locals_[2].start()

    def remote(src, dst, send, recv, dev):
        return pltpu.make_async_remote_copy(
            src_ref=src, dst_ref=dst, send_sem=send, recv_sem=recv, device_id=dev, device_id_type=MESH
        )

    def halo_copies(step, j):
        target = (field0, field1)[step]
        ls = levels_of(j)
        if step == 0:
            low_src = tracers.at[:, ls, pl.ds(0, RIM), :]
            high_src = tracers.at[:, ls, pl.ds(width_x - RIM, RIM), :]
        else:
            low_src = field1.at[:, ls, pl.ds(GROUP, RIM), :]
            high_src = field1.at[:, ls, pl.ds(GROUP + width_x - RIM, RIM), :]
        return (
            remote(
                high_src,
                target.at[:, ls, pl.ds(GROUP - RIM, RIM), :],
                halo_send.at[step, j, 0],
                halo_recv.at[step, j, 0],
                device(0, 1, 0),
            ),
            remote(
                low_src,
                target.at[:, ls, pl.ds(width_x + GROUP, RIM), :],
                halo_send.at[step, j, 1],
                halo_recv.at[step, j, 1],
                device(0, -1, 0),
            ),
        )

    def pack_copies(step, j):
        turned = (turned0, turned1)[step]
        ps = pairs_of(j)
        return (
            remote(
                turned.at[:, ps, pl.ds(GROUP + width_y - RIM, RIM), :],
                turned.at[:, ps, pl.ds(GROUP - RIM, RIM), :],
                pack_send.at[step, j, 0],
                pack_recv.at[step, j, 0],
                device(0, 0, 1),
            ),
            remote(
                turned.at[:, ps, pl.ds(GROUP, RIM), :],
                turned.at[:, ps, pl.ds(GROUP + width_y, RIM), :],
                pack_send.at[step, j, 1],
                pack_recv.at[step, j, 1],
                device(0, 0, -1),
            ),
        )

    halos = [[halo_copies(step, j) for j in range(4)] for step in range(2)]
    packs = [[pack_copies(0, j) for j in range(4)], [() for j in range(4)]]
    above = pl.ds(0, RIM)
    below = pl.ds(GROUP - RIM, RIM)

    def rim_pair(src, dst, n, dx):
        return [
            remote(
                src.at[..., rows, :], dst.at[..., rows, :], rim_send.at[n + i], rim_recv.at[n + i], device(0, dx, dy)
            )
            for i, (rows, dy) in enumerate(((below, 1), (above, -1)))
        ]

    flux_sends = rim_pair(rim_flux, far_flux, 0, 0)
    rim_sends = []
    for t in range(trac):
        first = 2 + 6 * t
        sends = rim_pair(corner.at[t], far_corner.at[0, t], first + 2, 1)
        sends += rim_pair(rim_after.at[t], far_rim.at[t], first, 0)
        if n_x > 2:
            sends += rim_pair(corner.at[t], far_corner.at[1, t], first + 4, -1)
        rim_sends.append(sends)

    lane = lax.broadcasted_iota(jnp.int32, (GROUP, LANES), 1)
    first_half = lane < width_x
    across = lax.rem(lane, width_x)
    slot = lax.rem(lane + LANES - (width_x - RIM), width_x)
    upper_rows = lax.broadcasted_iota(jnp.int32, (GROUP, LANES), 0) < GROUP // 2
    n_pairs = levels // 2
    y_groups = tuple(range(width_y // GROUP))

    def rim_of(tile):
        return jnp.where(upper_rows, tile[:GROUP], tile[width_y - GROUP :])

    def turn_flux_rims():
        def one_pair(p, carry):
            for u in range(2):
                both = fx[pl.ds(2 * p, 2), pl.ds(GROUP - 1 + u, width_x), :]
                rim_flux[u, p] = rim_of(both.reshape(2 * width_x, width_y).T)
            return carry

        lax.fori_loop(0, n_pairs, one_pair, 0)

    def rim_taps():
        for p in range(n_pairs):
            taps = cell_taps(face_weights(far_flux[0, p]), face_weights(far_flux[1, p]))
            for k in range(TAPS):
                far_taps[k, p] = taps[k]

    def turn_wind_rims(j):
        for n in range(pairs):
            p = member_of(j) * pairs + n
            rim_winds[p] = rim_of(fz[pl.ds(2 * p, 2)].reshape(2 * width_x, width_y).T)

    def rim_sweep_z():
        winds_at = [rim_winds[p] for p in range(n_pairs)]
        winds_at[-1] = jnp.where(first_half, winds_at[-1], 0.0)

        def swap(x):
            return pltpu.roll(x, width_x, 1)

        for t in range(trac):
            q = [rim_before[t, p] for p in range(n_pairs)]
            r = [swap(x) for x in q]
            top = jnp.where(first_half, q[0], r[0])
            bottom = jnp.where(first_half, r[-1], q[-1])

            def at(rows, p):
                return top if p < 0 else bottom if p >= n_pairs else rows[p]

            def next_level(p):
                return jnp.where(first_half, at(r, p), at(r, p + 1))

            flows = []
            for p in range(n_pairs):
                cells = [
                    at(q, p - 1),
                    jnp.where(first_half, at(r, p - 1), r[p]),
                    q[p],
                    next_level(p),
                    at(q, p + 1),
                    next_level(p + 1),
                ]
                flows.append(weighted(face_weights(winds_at[p]), cells))
            turned_flows = [swap(f) for f in flows]
            packed = None
            for p in range(n_pairs):
                earlier = turned_flows[p - 1] if p else jnp.zeros_like(top)
                new = q[p] + (jnp.where(first_half, earlier, turned_flows[p]) - flows[p])
                rim_after[t, p] = new
                moved = pltpu.roll(new, GROUP * p, 1) if p else new
                packed = moved if packed is None else jnp.where(slot // GROUP == p, moved, packed)
            corner[t] = packed
            for c in rim_sends[t]:
                c.start()

    def rim_sweep_x():
        for t in range(trac):
            for c in rim_sends[t]:
                c.wait_recv()
            beyond = far_corner[0, t]
            if n_x > 2:
                beyond = jnp.where(lax.rem(slot, GROUP) < RIM, beyond, far_corner[1, t])
            for p in range(n_pairs):
                own = far_rim[t, p]
                other = pltpu.roll(beyond, (width_x - GROUP * p) % LANES, 1)
                cells = []
                for d in range(-RIM, RIM + 1):
                    if d == 0:
                        cells.append(own)
                        continue
                    inside = (across + d >= 0) & (across + d < width_x)
                    cells.append(
                        jnp.where(inside, pltpu.roll(own, -d % LANES, 1), pltpu.roll(other, -d % LANES, 1))
                    )
                new = weighted([far_taps[k, p] for k in range(TAPS)], cells)
                turned1[t, p, pl.ds(GROUP - RIM, RIM), :] = new[GROUP - RIM :]
                turned1[t, p, pl.ds(GROUP + width_y, RIM), :] = new[:RIM]

    direct = [
        [
            remote(wind_src(k), wind_dst(k, 0), wind_send.at[j - 1, k], wind_recv.at[j - 1, k], device(j, 0, 0))
            for k in range(len(parts))
        ]
        for j in (1, 2)
    ]
    tail = len(parts) - 1
    relay = [
        remote(wind_dst(k, 2), wind_dst(k, 2), wind_send.at[2, k], wind_recv.at[2, k], device(1, 0, 0))
        for k in range(tail)
    ]
    relay.append(
        remote(
            wind_src(tail), wind_dst(tail, 0), wind_send.at[2, tail], wind_recv.at[2, tail], device(3, 0, 0)
        )
    )

    x_edges = [
        remote(
            flux_x.at[:, pl.ds(width_x - 1, 1), :],
            fx.at[levels_of(0), pl.ds(GROUP - 1, 1), :],
            edge_send.at[0, j],
            edge_recv.at[0, j],
            device(j, 1, 0),
        )
        for j in range(4)
    ]
    y_edges = [
        remote(
            fyt.at[pairs_of(0), pl.ds(GROUP + width_y - 1, 1), :],
            fyt.at[pairs_of(0), pl.ds(GROUP - 1, 1), :],
            edge_send.at[1, j],
            edge_recv.at[1, j],
            device(j, 0, 1),
        )
        for j in range(4)
    ]

    def turn_wind(j):
        first = member_of(j) * pairs

        def one_pair(k, carry):
            p = first + k
            both = fy[pl.ds(2 * p, 2)].reshape(2 * width_x, width_y)
            fyt[p, pl.ds(GROUP, width_y), :] = both.T
            return carry

        lax.fori_loop(0, pairs, one_pair, 0)

    def put_faces(read, start, row):
        for k, w in enumerate(face_weights(read(start))):
            face[k, pl.ds(row, GROUP), :] = w

    def put_taps(store, g, row):
        low = [face[k, pl.ds(row, GROUP), :] for k in range(FACE)]
        high = [face[k, pl.ds(row + 1, GROUP), :] for k in range(FACE)]
        for k, tap in enumerate(cell_taps(low, high)):
            store(k, g, tap)

    def inner_taps(read, store, extent):
        for g in range(extent // GROUP):
            put_faces(read, GROUP * g + 1, GROUP * g + GROUP)
        for g in range(1, extent // GROUP):
            put_taps(store, g, GROUP * g + GROUP - 1)

    def first_taps(read, store):
        put_faces(read, 0, 0)
        put_faces(read, 1, 1)
        put_taps(store, 0, 0)

    def x_taps(j, inside):
        first = member_of(j) * slab

        def one_level(n, carry):
            level = first + n

            def read(start):
                return fx[level, pl.ds(GROUP - 1 + start, GROUP), :]

            def store(k, g, tap):
                vx[k, level, pl.ds(GROUP * g, GROUP), :] = tap

            if inside:
                inner_taps(read, store, width_x)
            else:
                first_taps(read, store)
            return carry

        lax.fori_loop(0, slab, one_level, 0)

    def y_taps(j, inside):
        first = member_of(j) * pairs

        def one_pair(n, carry):
            p = first + n

            def read(start):
                return fyt[p, pl.ds(GROUP - 1 + start, GROUP), :]

            def store(k, g, tap):
                vy[k, p, pl.ds(GROUP * g, GROUP), :] = tap

            if inside:
                inner_taps(read, store, width_y)
            else:
                first_taps(read, store)
            return carry

        lax.fori_loop(0, pairs, one_pair, 0)

    locals_[1].wait()
    turn_wind(0)
    pl.semaphore_wait(barrier, len(near) + lax.min(iy, 1) + lax.min(last - iy, 1))
    signal(known.at[0], (0, -1, 0))
    pl.when(iy > 0)(lambda: signal(known.at[1], down))
    pl.when(iy == 0)(lambda: signal(far.at[1], up))
    pl.when(iy == last - 1)(lambda: signal(far.at[0], down))
    direct[1][0].start()
    x_edges[0].start()
    for c in halos[0][0]:
        c.start()
    direct[0][0].start()
    for j in range(1, 4):
        for c in halos[0][j]:
            c.start()

    locals_[0].wait()
    x_taps(0, True)
    y_taps(0, True)

    pl.semaphore_wait(known.at[0], 1)
    for c in x_edges[1:]:
        c.start()

    @pl.when(iy < last)
    def _():
        pl.semaphore_wait(known.at[1], 1)
        for c in y_edges:
            c.start()

    for k in range(1, len(parts)):
        direct[1][k].start()
        direct[0][k].start()
    relay[tail].start()

    @pl.when((iy > 0) & (iy < last - 1))
    def _():
        pl.semaphore_wait(far.at[0], 1)
        signal(far.at[0], down)

    @pl.when((iy > 0) & (iy < last))
    def _():
        pl.semaphore_wait(far.at[1], 1)
        signal(far.at[1], up)

    def ends_are_in():
        @pl.when(iy == 0)
        def _():
            pl.semaphore_wait(far.at[0], 1)

        @pl.when(iy == last)
        def _():
            pl.semaphore_wait(far.at[1], 1)
            for c in y_edges:
                c.start()

    def wait_wind(k, j):
        if j == 3:
            relay[k].wait_recv()
        else:
            direct[j - 1][k].wait_recv()

    def sweep_x(step, j):
        field = (field0, field1)[step]
        turned = (turned0, turned1)[step]
        for n in range(pairs):
            p = member_of(j) * pairs + n
            for h in range(2):
                level = 2 * p + h
                for g in range(width_x // GROUP):
                    taps = [vx[k, level, pl.ds(GROUP * g, GROUP), :] for k in range(TAPS)]
                    for t in range(trac):
                        cells = [
                            field[t, level, pl.ds(GROUP + GROUP * g + s, GROUP), :] for s in range(-RIM, RIM + 1)
                        ]
                        swept[pairs * j + n, t, pl.ds(width_x * h + GROUP * g, GROUP), :] = weighted(taps, cells)
            for t in range(trac):
                turned[t, p, pl.ds(GROUP, width_y), :] = swept[pairs * j + n, t].T

    def sweep_y(step, j, groups):
        turned = (turned0, turned1)[step]
        for n in range(pairs):
            p = member_of(j) * pairs + n
            for g in groups:
                taps = [vy[k, p, pl.ds(GROUP * g, GROUP), :] for k in range(TAPS)]
                for t in range(trac):
                    cells = [turned[t, p, pl.ds(GROUP + GROUP * g + s, GROUP), :] for s in range(-RIM, RIM + 1)]
                    swept[pairs * j + n, t, pl.ds(GROUP * g, GROUP), :] = weighted(taps, cells)

    def turn_back(step, j):
        for n in range(pairs):
            p = member_of(j) * pairs + n
            for t in range(trac):
                done = swept.at[pairs * j + n, t]
                if step == 0:
                    rim_before[t, p] = jnp.where(
                        upper_rows, done[pl.ds(0, GROUP), :], done[pl.ds(width_y - GROUP, GROUP), :]
                    )
                (mid, field_out)[step][t, pl.ds(2 * p, 2)] = done[...].T.reshape(2, width_x, width_y)

    def sweep_z(row):
        def put(t, l, new):
            field1[t, l, pl.ds(GROUP + row, GROUP), :] = new

        column_sweep(mid, fz, row, put)

    def exchange(k):
        direct[1][k].wait_recv()
        relay[k].start()

    wait_wind(0, 1)
    x_taps(1, True)
    load.wait()
    for j in range(4):
        if j == 2:
            exchange(0)
        if j == 3:
            wait_wind(0, 3)
        if j > 1:
            x_taps(j, True)
        x_edges[j].wait_recv()
        x_taps(j, False)
        for c in halos[0][j]:
            c.wait_recv()
        sweep_x(0, j)
        if j == 0:
            ends_are_in()
        for c in packs[0][j]:
            c.start()
        if j == 0:
            wait_wind(1, 1)
            turn_wind(1)
            y_taps(1, True)
    turn_flux_rims()
    for c in flux_sends:
        c.start()
    for j in range(4):
        if j == 1:
            exchange(1)
            turn_wind(2)
            y_taps(2, True)
        if j == 2:
            wait_wind(1, 3)
            turn_wind(3)
            y_taps(3, True)
            exchange(2)
            exchange(3)
            locals_[2].wait()
            turn_wind_rims(0)
            for k in (2, 3, 4, tail):
                wait_wind(k, 1)
            turn_wind_rims(1)
        sweep_y(0, j, y_groups[1:-1])
    for j in range(4):
        y_edges[j].wait_recv()
        y_taps(j, False)
        for c in packs[0][j]:
            c.wait_recv()
        sweep_y(0, j, (y_groups[0], y_groups[-1]))
        turn_back(0, j)
    for k in (2, 3):
        wait_wind(k, 3)
    sweep_z(0)
    sweep_z(width_x - GROUP)
    for j in range(4):
        for c in halos[1][j]:
            c.start()
    exchange(4)
    wait_wind(tail, 2)
    turn_wind_rims(2)
    wait_wind(4, 3)
    wait_wind(tail, 3)
    turn_wind_rims(3)
    rim_sweep_z()
    winds_on = pltpu.make_async_copy(fz, winds_out, out_sem)
    winds_on.start()

    def one_group(g, carry):
        sweep_z(pl.multiple_of(g * GROUP, GROUP))
        return carry

    lax.fori_loop(1, width_x // GROUP - 1, one_group, 0)

    for c in flux_sends:
        c.wait_recv()
    rim_taps()
    for j in range(4):
        for c in halos[1][j]:
            c.wait_recv()
        sweep_x(1, j)
        sweep_y(1, j, y_groups[1:-1])
    rim_sweep_x()
    for j in range(4):
        sweep_y(1, j, (y_groups[0], y_groups[-1]))
        turn_back(1, j)
    winds_on.wait()

    for step in range(2):
        for j in range(4):
            for c in halos[step][j] + packs[step][j]:
                c.wait_send()
    for c in direct[0] + direct[1] + relay + x_edges + y_edges + flux_sends + sum(rim_sends, []):
        c.wait_send()


def body(sizes, tracers, flux_x, flux_y, flux_z):
    trac, levels, width_x, width_y = tracers.shape
    members = sizes[0]
    padded = pltpu.VMEM((trac, levels, width_x + 2 * GROUP, width_y), jnp.float32)
    turned = pltpu.VMEM((trac, levels // 2, width_y + 2 * GROUP, 2 * width_x), jnp.float32)
    rims = pltpu.VMEM((trac, levels // 2, GROUP, LANES), jnp.float32)
    flux_rims = pltpu.VMEM((2, levels // 2, GROUP, LANES), jnp.float32)
    block = pltpu.VMEM((levels, width_x, width_y), jnp.float32)
    swept, winds = pl.pallas_call(
        functools.partial(kernel, sizes),
        out_shape=[
            pltpu.VMEM(tracers.shape, jnp.float32),
            pltpu.VMEM((levels, width_x, width_y), jnp.float32),
        ],
        in_specs=[pl.BlockSpec(memory_space=pltpu.HBM)] * 4,
        out_specs=[pl.BlockSpec(memory_space=pltpu.VMEM)] * 2,
        scratch_shapes=[
            padded,
            padded,
            turned,
            turned,
            pltpu.VMEM((trac, levels, width_x, width_y), jnp.float32),
            pltpu.VMEM((levels, width_x + GROUP, width_y), jnp.float32),
            block,
            block,
            pltpu.VMEM((levels // 2, width_y + GROUP, 2 * width_x), jnp.float32),
            pltpu.VMEM((TAPS, levels, width_x, width_y), jnp.float32),
            pltpu.VMEM((TAPS, levels // 2, width_y, 2 * width_x), jnp.float32),
            pltpu.VMEM((FACE, width_y + GROUP, LANES), jnp.float32),
            pltpu.VMEM((levels // 2, trac, 2 * width_x, width_y), jnp.float32),
            rims,
            rims,
            flux_rims,
            flux_rims,
            rims,
            pltpu.VMEM((trac, GROUP, LANES), jnp.float32),
            pltpu.VMEM((2, trac, GROUP, LANES), jnp.float32),
            pltpu.VMEM((TAPS, levels // 2, GROUP, LANES), jnp.float32),
            pltpu.VMEM((levels // 2, GROUP, LANES), jnp.float32),
            pltpu.SemaphoreType.DMA((4,)),
            pltpu.SemaphoreType.DMA((3, 6)),
            pltpu.SemaphoreType.DMA((3, 6)),
            pltpu.SemaphoreType.DMA((2, 4)),
            pltpu.SemaphoreType.DMA((2, 4)),
            pltpu.SemaphoreType.DMA((2, 4, 2)),
            pltpu.SemaphoreType.DMA((2, 4, 2)),
            pltpu.SemaphoreType.DMA((2, 4, 2)),
            pltpu.SemaphoreType.DMA((2, 4, 2)),
            pltpu.SemaphoreType.DMA,
            pltpu.SemaphoreType.REGULAR((2,)),
            pltpu.SemaphoreType.REGULAR((2,)),
            pltpu.SemaphoreType.DMA((14,)),
            pltpu.SemaphoreType.DMA((14,)),
        ],
        compiler_params=pltpu.CompilerParams(
            collective_id=0, has_side_effects=True, vmem_limit_bytes=40 * 2**20
        ),
    )(*(pltpu.with_memory_space_constraint(a, pltpu.HBM) for a in (tracers, flux_x, flux_y, flux_z)))
    return pl.pallas_call(
        last_kernel,
        out_shape=jax.ShapeDtypeStruct(tracers.shape, jnp.float32),
        in_specs=[pl.BlockSpec(memory_space=pltpu.VMEM)] * 2,
        out_specs=pl.BlockSpec(memory_space=pl.ANY),
        scratch_shapes=[
            pltpu.VMEM(tracers.shape, jnp.float32),
            pltpu.SemaphoreType.DMA((width_x // GROUP,)),
        ],
        compiler_params=pltpu.CompilerParams(vmem_limit_bytes=8 * 2**20),
    )(swept, winds)


def solution(mesh):
    sizes = (mesh.shape["member"], mesh.shape["gx"], mesh.shape["gy"])
    return jax.shard_map(
        functools.partial(body, sizes),
        mesh=mesh,
        in_specs=(
            P("member", None, "gx", "gy"),
            P("member", "gx", "gy"),
            P("member", "gx", "gy"),
            P("member", "gx", "gy"),
        ),
        out_specs=P("member", None, "gx", "gy"),
        check_vma=False,
    )
```
